32 devices in a mesh: ia: 4 (over z), ja: 4 (over y, core), ka: 2 (over x).
Axes of the slice: x: 2, y: 2, z: 4, core: 2. Of those that a mesh axis runs over, the one named last changes fastest.
Arguments:
- tensor: float32 [8192, 8, 1024], P('ja', 'ka', 'ia'), may hold values from -6 to 6
- factor_a: float32 [1024, 128], P('ia'), may hold values from -1 to 1
- factor_c: float32 [8, 128], P('ka'), may hold values from -2 to 2
- gram_c: float32 [128, 128], replicated, may hold values from -12 to 24, as said below
Outputs:
- factor_b: float32 [8192, 128], P('ja')
- factor_c_new: float32 [8, 128], P('ka')
The draws below stay inside these ranges and needn't reach their ends.
Inputs may be any that keep to these rules, and one draw needn't show every extreme that they name: `gram_c`: symmetric positive definite.
All inputs are finite; a program needn't handle non-finite values.
Results may differ from the reference program's by a relative error of at most 0.000071.
Values sent between devices are 32-bit elements; how exact they have to be, the bound alone decides.
A program may use at most 64 MiB of HBM per device.

```python
import jax
import jax.numpy as jnp
from jax import lax

R = 128
I = 1024
J = 8192
K = 8


def draw_factor_a(key, part):
    first, second, third = jax.random.split(jax.random.fold_in(key, 11), 3)
    noise = jnp.clip(jax.random.normal(first, (I, R), jnp.float32), -4.0, 4.0)
    common = jnp.clip(jax.random.normal(second, (I, 1), jnp.float32), -4.0, 4.0)
    weights = jnp.clip(jax.random.normal(third, (1, R), jnp.float32), -4.0, 4.0)
    return ((noise + 0.7 * common * weights) / jnp.sqrt(jnp.float32(I))).astype(jnp.float32)


def draw_gram_c(key, part):
    first, second = jax.random.split(jax.random.fold_in(key, 23), 2)
    mixing = jnp.clip(jax.random.normal(first, (R, R), jnp.float32), -4.0, 4.0)
    shared = jnp.clip(jax.random.normal(second, (R,), jnp.float32), -3.0, 3.0)
    result = 0.5 * jnp.eye(R, dtype=jnp.float32) + jnp.dot(mixing, mixing.T) / R + 0.3 * jnp.outer(shared, shared)
    return jnp.clip(result, -12.0, 24.0).astype(jnp.float32)


def block_scale(stream_key, extent, pieces, smallest, high):
    def one(axis_at, parts):
        steps = jax.random.uniform(jax.random.fold_in(jax.random.fold_in(stream_key, 6), axis_at), (parts,), jnp.float32, smallest / len(pieces), high / len(pieces))
        return jnp.repeat(jnp.exp(steps), extent[axis_at] // parts).reshape((-1,) + (1,) * (len(extent) - axis_at - 1))

    loudness = one(*pieces[0])
    for cut in pieces[1:]:
        loudness = loudness * one(*cut)
    return loudness


def bell_draw(rng, shape, scale, bound, cuts=(), kind=jnp.bfloat16):
    values = jax.random.normal(rng, shape, jnp.float32) * scale
    if len(cuts) > 0:
        values = block_scale(rng, shape, cuts, -0.22, 0.18) * values
    return jnp.clip(values, min=-bound, max=bound).astype(kind)


def setup_inputs(seed: int = 0) -> dict:
    arg_keys = jax.random.split(jax.random.key(seed), 5)
    tensor = bell_draw(arg_keys[0], (J, K, I), 1.0, 6.0, ((0, 4), (1, 2), (2, 4)), jnp.float32)
    factor_a = draw_factor_a(jax.random.fold_in(arg_keys[4], 71), 0)
    factor_c = bell_draw(arg_keys[2], (K, R), K ** -0.5, 2.0, ((0, 2),), jnp.float32)
    gram_c = draw_gram_c(jax.random.fold_in(arg_keys[4], 71), 0)
    return {"tensor": tensor, "factor_a": factor_a, "factor_c": factor_c, "gram_c": gram_c}


def right_solve(rhs, system):
    lower = jnp.linalg.cholesky(system)
    middle = lax.linalg.triangular_solve(lower, rhs, left_side=False, lower=True, transpose_a=True)
    return lax.linalg.triangular_solve(lower, middle, left_side=False, lower=True, transpose_a=False)

def reference(tensor, factor_a, factor_c, gram_c):
    high = lax.Precision.HIGHEST
    partial_value = jnp.dot(tensor.reshape(J * K, I).astype(jnp.float32), factor_a.astype(jnp.float32), precision=high, preferred_element_type=jnp.float32).reshape(J, K, R)
    gram_a = jnp.dot(factor_a.T.astype(jnp.float32), factor_a.astype(jnp.float32), precision=high, preferred_element_type=jnp.float32)
    mttkrp_b = jnp.sum(partial_value * factor_c[None, :, :], axis=1)
    factor_b = right_solve(mttkrp_b, gram_a * gram_c)
    mttkrp_c = jnp.sum(partial_value * factor_b[:, None, :], axis=0)
    gram_b = jnp.dot(factor_b.T.astype(jnp.float32), factor_b.astype(jnp.float32), precision=high, preferred_element_type=jnp.float32)
    factor_c_new = right_solve(mttkrp_c, gram_a * gram_b)
    return (factor_b, factor_c_new)
```

```python
import functools

import jax
import jax.numpy as jnp
from jax import lax
from jax.experimental import pallas as pl
from jax.experimental.pallas import tpu as pltpu
from jax.sharding import PartitionSpec as P

HIGH = lax.Precision.HIGHEST
MESH = pl.DeviceIdType.MESH
PANEL = 64
WARM, FIRST, BEGIN, X_TIME, HOP = 2.0, 3.7, 3.0, 11.4, 2.5
LAG = (2.2, 3.0, 2.9, 2.3, 0.0)
REDUCE_AT, GRAM_AT, UNIT = 6.3, 9.5, 0.35
PIECE = 8


def mm(a, b):
    return jnp.dot(a, b, precision=HIGH, preferred_element_type=jnp.float32)


def split3(x):
    a = x.astype(jnp.bfloat16)
    x = x - a.astype(jnp.float32)
    b = x.astype(jnp.bfloat16)
    c = (x - b.astype(jnp.float32)).astype(jnp.bfloat16)
    return a, b, c


def pack_right(w):
    b1, b2, b3 = split3(w)
    top = jnp.concatenate([b1, b2], axis=1)
    return jnp.concatenate([top, top], axis=0), jnp.concatenate([b1, b3], axis=0)


def mm_packed(x, first, second):
    n = second.shape[1]
    a1, a2, a3 = split3(x)
    y = jnp.dot(jnp.concatenate([a1, a2], axis=1), first, preferred_element_type=jnp.float32)
    z = jnp.dot(jnp.concatenate([a3, a1], axis=1), second, preferred_element_type=jnp.float32)
    return y[:, :n] + (y[:, n:] + z)


def mtm(a):
    return lax.dot_general(
        a, a, (((0,), (0,)), ((), ())), precision=HIGH, preferred_element_type=jnp.float32
    )


def take_pivots(rows, q, at):
    n = rows[0].shape[1]
    lane = lax.broadcasted_iota(jnp.int32, (PIECE, n), 1)
    sub = lax.broadcasted_iota(jnp.int32, (PIECE, n), 0)
    lane_row = lax.broadcasted_iota(jnp.int32, (1, n), 1)
    order = [q] + [v for v in range(len(rows)) if v != q]
    cols = {
        v: [jnp.broadcast_to(rows[v][:, at + j : at + j + 1], (PIECE, n)) for j in range(PIECE)]
        for v in order
    }
    x, ahead = rows[q], list(cols[q])
    for t in range(0, PIECE, 2):
        c0, c1 = ahead[t], ahead[t + 1]
        p, r = c0[t : t + 1], c1[t : t + 1]
        u, s = c0[t + 1 : t + 2], c1[t + 1 : t + 2]
        inv = 1.0 / (p * s - r * u)

        def step(y0, y1, kept):
            w0 = (s * y0 - r * y1) * inv
            w1 = (p * y1 - u * y0) * inv
            rest = kept - c0 * w0 - c1 * w1
            return jnp.where(sub == t, w0, jnp.where(sub == t + 1, w1, rest))

        for j in range(t + 2, PIECE):
            y = ahead[j]
            ahead[j] = step(y[t : t + 1], y[t + 1 : t + 2], y)
        here, there = lane_row == at + t, lane_row == at + t + 1
        y0 = jnp.where(here, 1.0, jnp.where(there, 0.0, x[t : t + 1]))
        y1 = jnp.where(here, 0.0, jnp.where(there, 1.0, x[t + 1 : t + 2]))
        x = step(y0, y1, jnp.where((lane == at + t) | (lane == at + t + 1), 0.0, x))
    own = (lane >= at) & (lane < at + PIECE)
    out = list(rows)
    out[q] = x
    for v in order[1:]:
        terms = [cols[v][j] * x[j : j + 1] for j in range(PIECE)]
        while len(terms) > 1:
            terms = [terms[i] + terms[i + 1] for i in range(0, len(terms), 2)]
        out[v] = jnp.where(own, 0.0, rows[v]) - terms[0]
    return out


def inverse_steps(a):
    n = a.shape[0]
    lane = lax.broadcasted_iota(jnp.int32, (n, n), 1)
    sub = lax.broadcasted_iota(jnp.int32, (n, n), 0)
    for base in range(0, n, PANEL):
        rows = [a[base + m : base + m + PIECE] for m in range(0, PANEL, PIECE)]
        for q in range(len(rows)):
            rows = take_pivots(rows, q, base + PIECE * q)
            if q + 1 < len(rows):
                yield None
        pieces = [jnp.zeros((base, n), jnp.float32)] if base else []
        pieces += rows
        if base + PANEL < n:
            pieces.append(jnp.zeros((n - base - PANEL, n), jnp.float32))
        done = jnp.concatenate(pieces, axis=0)
        inside = (lane >= base) & (lane < base + PANEL)
        factor = jnp.where(inside, a, 0.0)
        rest = jnp.where(inside, 0.0, a) - mm_packed(factor, *pack_right(done))
        a = jnp.where((sub >= base) & (sub < base + PANEL), done, rest)
        yield a


def inverse(a):
    for a in inverse_steps(a):
        pass
    return a


def plan(blocks, units):
    pace = X_TIME / blocks
    events = []
    ready = [0.0] * blocks
    for b in range(blocks):
        events.append((WARM + FIRST / blocks * (b + 1), b, "first", b))
        t = BEGIN + pace * (b + 1) + HOP
        for n, name in enumerate(("second", "reduce_more", "third", "gather_more", "fourth")):
            events.append((t, b, name, b))
            ready[b] = t
            t += LAG[n]
    link = BEGIN + X_TIME
    for b in range(blocks):
        link = max(link, ready[b]) + pace
        events.append((link + HOP, b, "fifth", b))
    events.append((REDUCE_AT, blocks, "gram_reduce", None))
    for n in range(units):
        events.append((GRAM_AT + n * UNIT, blocks, "side", None))
    return [(name, b) for _, _, name, b in sorted(events, key=lambda e: e[:2])]


def scales(h):
    n = h.shape[0]
    eye = lax.broadcasted_iota(jnp.int32, (n, n), 1) == lax.broadcasted_iota(jnp.int32, (n, n), 0)
    kept = jnp.where(eye, h, 0.0)
    across = lax.rsqrt(jnp.sum(kept, axis=0, keepdims=True))
    down = lax.rsqrt(jnp.sum(kept, axis=1, keepdims=True))
    return down, across


def kernel(
    dims,
    blocks,
    t_hbm,
    a_hbm,
    c_hbm,
    gc_hbm,
    b_out,
    c_out,
    tbuf,
    part,
    mloc,
    xrecv,
    xsum,
    zrecv,
    mfull,
    bfull,
    ga_loc,
    ga_in,
    ga_full,
    g1,
    g_in,
    g_out,
    g3,
    mc_all,
    inv_a,
    inv_b,
    acc_ref,
    a_ref,
    c_ref,
    gc_ref,
    t_sem,
    x_send,
    x_recv,
    z_send,
    z_recv,
    p_send,
    p_recv,
    q_send,
    q_recv,
    ga_send,
    ga_recv,
    gf_send,
    gf_recv,
    g_send,
    g_recv,
    mc_send,
    mc_recv,
    o_sem,
    i_sem,
):
    ni, nj, nk = dims
    kl, rows, rank = part.shape
    jb = rows // blocks
    jx = jb // nk
    jz = jx // ni
    mi, mj, mk = lax.axis_index("ia"), lax.axis_index("ja"), lax.axis_index("ka")
    sends = []

    def peer(axis, me, n, d):
        return {axis: lax.rem(me + d, n)}

    def remote(src, dst, ss, rs, who):
        cp = pltpu.make_async_remote_copy(
            src_ref=src, dst_ref=dst, send_sem=ss, recv_sem=rs, device_id=who, device_id_type=MESH
        )
        cp.start()
        sends.append(cp)
        return cp

    icopies = []
    for n, (src, dst) in enumerate(((a_hbm, a_ref), (c_hbm, c_ref), (gc_hbm, gc_ref))):
        cp = pltpu.make_async_copy(src, dst, i_sem.at[n])
        cp.start()
        icopies.append(cp)
    tcopies = {}
    for b in range(blocks):
        for k in range(kl):
            rs = pl.ds(b * jb, jb)
            cp = pltpu.make_async_copy(t_hbm.at[rs, k, :], tbuf.at[k, rs, :], t_sem.at[b, k])
            cp.start()
            tcopies[b, k] = cp

    barrier = pltpu.get_barrier_semaphore()
    for d in range(1, ni):
        pl.semaphore_signal(barrier, inc=1, device_id=peer("ia", mi, ni, d), device_id_type=MESH)
    for d in range(1, nj):
        pl.semaphore_signal(barrier, inc=1, device_id=peer("ja", mj, nj, d), device_id_type=MESH)
    for d in range(1, nk):
        pl.semaphore_signal(barrier, inc=1, device_id=peer("ka", mk, nk, d), device_id_type=MESH)

    for cp in icopies:
        cp.wait()
    a = a_ref[...]
    a_hi = a.astype(jnp.bfloat16)
    a_lo = (a - a_hi.astype(jnp.float32)).astype(jnp.bfloat16)
    weights = jnp.concatenate([a_hi, a_lo], axis=1)
    ga_loc[...] = mtm(a)

    x_cp, z_cp, p_cp, q_cp = {}, {}, {}, {}
    step = min(256, jb)

    def first(b):
        for k in range(kl):
            tcopies[b, k].wait()

        def chunk(s, carry):
            rs = pl.ds(pl.multiple_of(b * jb + s * step, step), step)
            total = None
            for k in range(kl):
                x = tbuf[k, rs, :]
                hi = x.astype(jnp.bfloat16)
                lo = (x - hi.astype(jnp.float32)).astype(jnp.bfloat16)
                y = jnp.dot(hi, weights, preferred_element_type=jnp.float32) + jnp.dot(
                    lo, weights, preferred_element_type=jnp.float32
                )
                y = y[:, :rank] + y[:, rank:]
                part[k, rs, :] = y
                y = y * c_ref[k : k + 1, :]
                total = y if total is None else total + y
            mloc[rs, :] = total
            return carry

        lax.fori_loop(0, jb // step, chunk, 0)

    def send_first(b):
        for d in range(1, nk):
            other = lax.rem(mk + d, nk)
            rs = pl.ds(pl.multiple_of(b * jb + other * jx, 8), jx)
            x_cp[b, d] = remote(
                mloc.at[rs, :], xrecv.at[b, d - 1], x_send.at[b, d - 1], x_recv.at[b, d - 1],
                peer("ka", mk, nk, d),
            )

    hops = []
    while 2 ** len(hops) < ni:
        hops.append(2 ** len(hops))
    levels = len(hops)
    bits = [lax.rem(lax.div(mi, m), 2) for m in hops]
    starts, arrive = [0], [0]
    for n in range(levels):
        starts.append(starts[n] + bits[n] * (jx >> (n + 1)))
        arrive.append(arrive[n] + (jx >> (n + 1)))

    def across_ia(n):
        return {"ia": mi + hops[n] * (1 - 2 * bits[n])}

    def z_start(b, n):
        size = jx >> (n + 1)
        give = pl.ds(pl.multiple_of(starts[n] + (1 - bits[n]) * size, 8), size)
        z_cp[b, n] = remote(
            xsum.at[b, give, :], zrecv.at[b, pl.ds(arrive[n], size), :], z_send.at[b, n],
            z_recv.at[b, n], across_ia(n),
        )

    def z_finish(b, n):
        size = jx >> (n + 1)
        z_cp[b, n].wait_recv()
        keep = pl.ds(pl.multiple_of(starts[n + 1], 8), size)
        return keep, xsum[b, keep, :] + zrecv[b, pl.ds(arrive[n], size), :]

    def p_start(b, n):
        rs = pl.ds(pl.multiple_of(b * jb + mk * jx + starts[n + 1], 8), jx >> (n + 1))
        p_cp[b, n] = remote(
            mfull.at[rs, :], mfull.at[rs, :], p_send.at[b, n], p_recv.at[b, n], across_ia(n)
        )

    def second(b):
        total = mloc[pl.ds(pl.multiple_of(b * jb + mk * jx, 8), jx), :]
        for d in range(1, nk):
            x_cp[b, d].wait_recv()
            total = total + xrecv[b, d - 1]
        xsum[b] = total
        z_start(b, 0)

    def reduce_more(b):
        for n in range(levels - 1):
            keep, value = z_finish(b, n)
            xsum[b, keep, :] = value
            z_start(b, n + 1)

    def third(b):
        _, total = z_finish(b, levels - 1)
        rs = pl.ds(pl.multiple_of(b * jb + mk * jx + starts[levels], 8), jz)
        mfull[rs, :] = total
        p_start(b, levels - 1)

    def gather_more(b):
        for n in range(levels - 1, 0, -1):
            p_cp[b, n].wait_recv()
            p_start(b, n - 1)

    def fourth(b):
        p_cp[b, 0].wait_recv()
        rs = pl.ds(pl.multiple_of(b * jb + mk * jx, 8), jx)
        for d in range(1, nk):
            q_cp[b, d] = remote(
                mfull.at[rs, :], mfull.at[rs, :], q_send.at[b, d - 1], q_recv.at[b, d - 1],
                peer("ka", mk, nk, d),
            )

    out_cp = []

    def fifth(b):
        for d in range(1, nk):
            q_cp[b, d].wait_recv()
        rs = pl.ds(b * jb, jb)
        value = mm_packed(mfull[rs, :], inv_a[...], inv_b[...])
        bfull[rs, :] = value
        gram = mtm(value)
        g1[...] = gram if b == 0 else g1[...] + gram
        return value

    def sixth(b, value):
        rs = pl.ds(b * jb, jb)
        for k in range(kl):
            s = jnp.sum(part[k, rs, :] * value, axis=0, keepdims=True)
            acc_ref[pl.ds(k, 1), :] = acc_ref[pl.ds(k, 1), :] + s
        cp = pltpu.make_async_copy(bfull.at[rs, :], b_out.at[rs, :], o_sem.at[b])
        cp.start()
        out_cp.append(cp)

    ahead = min(2, blocks)
    for b in range(ahead):
        first(b)
    pl.semaphore_wait(barrier, ni + nj + nk - 3)
    strip = rank // nj
    part_rows = pl.ds(pl.multiple_of(mj * strip, 8), strip)
    ga_in[mi] = ga_loc[part_rows, :]
    ga_cp = [
        remote(
            ga_loc.at[part_rows, :], ga_in.at[mi], ga_send.at[d - 1], ga_recv.at[d - 1],
            peer("ia", mi, ni, d),
        )
        for d in range(1, ni)
    ]
    for b in range(ahead):
        send_first(b)
    gf_cp = []
    state = {}

    def gram_reduce():
        for cp in ga_cp:
            cp.wait_recv()
        total = ga_in[0]
        for d in range(1, ni):
            total = total + ga_in[d]
        ga_full[part_rows, :] = total
        for d in range(1, nj):
            gf_cp.append(
                remote(
                    ga_full.at[part_rows, :], ga_full.at[part_rows, :], gf_send.at[d - 1],
                    gf_recv.at[d - 1], peer("ja", mj, nj, d),
                )
            )

    def side_steps():
        for cp in gf_cp:
            cp.wait_recv()
        h = ga_full[...] * gc_ref[...]
        down, across = scales(h)
        for h in inverse_steps(h * down * across):
            yield
        inv_a[...], inv_b[...] = pack_right(h * down * across)
        yield

    acc_ref[...] = jnp.zeros_like(acc_ref)
    units = rank // PIECE + 1
    side = side_steps()
    left = units

    def advance(count):
        for _ in range(count):
            next(side)

    for name, b in plan(blocks, units):
        if name == "first":
            if b >= ahead:
                first(b)
                send_first(b)
        elif name == "gram_reduce":
            gram_reduce()
        elif name == "side":
            if left:
                advance(1)
                left -= 1
        elif name == "fifth":
            advance(left)
            left = 0
            value = fifth(b)
            if b + 1 < blocks:
                sixth(b, value)
        else:
            {
                "second": second,
                "reduce_more": reduce_more,
                "third": third,
                "gather_more": gather_more,
                "fourth": fourth,
            }[name](b)

    half = rank // 2
    low = lax.rem(mj, 2)
    mine = pl.ds(pl.multiple_of(low * half, 8), half)
    other = pl.ds(pl.multiple_of((1 - low) * half, 8), half)
    partner = {"ja": mj + 1 - 2 * low}
    cp = remote(g1.at[other, :], g_in.at[0], g_send.at[0], g_recv.at[0], partner)
    sixth(blocks - 1, value)
    mc_all[mi * nj + mj] = acc_ref[...]
    mc_cp = []
    for d in range(ni):
        for e in range(nj):
            if d + e:
                where = {**peer("ia", mi, ni, d), **peer("ja", mj, nj, e)}
                n = d * nj + e - 1
                slot = mc_all.at[mi * nj + mj]
                mc_cp.append(remote(slot, slot, mc_send.at[n], mc_recv.at[n], where))
    cp.wait_recv()
    total = g1[mine, :] + g_in[0]
    level = 1
    while 2**level < nj:
        hop = 2**level
        bit = lax.rem(lax.div(mj, hop), 2)
        g_out[level - 1] = total
        cp = remote(
            g_out.at[level - 1], g_in.at[level], g_send.at[level], g_recv.at[level],
            {"ja": mj + hop * (1 - 2 * bit)},
        )
        cp.wait_recv()
        total = total + g_in[level]
        level += 1
    g3[mine, :] = total
    cp = remote(g3.at[mine, :], g3.at[mine, :], g_send.at[level], g_recv.at[level], partner)
    cp.wait_recv()
    h = ga_full[...] * g3[...]
    down, across = scales(h)
    h = h * down * across
    first_w, second_w = pack_right(inverse(h) * down * across)
    for cp in mc_cp:
        cp.wait_recv()
    mttkrp_c = mc_all[0]
    for n in range(1, ni * nj):
        mttkrp_c = mttkrp_c + mc_all[n]
    c_out[...] = mm_packed(mttkrp_c, first_w, second_w)[:kl, :]
    for cp in out_cp:
        cp.wait()
    for cp in sends:
        cp.wait_send()


def pass_on(pieces, b_in, c_in, b_out, c_out, b_ref, c_ref, load, store):
    size = b_ref.shape[0] // pieces
    cuts = [pl.ds(n * size, size) for n in range(pieces)]
    moves = [(b_in.at[cut, :], b_ref.at[cut, :], b_out.at[cut, :]) for cut in cuts]
    moves.insert(0, (c_in, c_ref, c_out))
    loads = [pltpu.make_async_copy(m[0], m[1], load.at[n]) for n, m in enumerate(moves)]
    stores = [pltpu.make_async_copy(m[1], m[2], store.at[n]) for n, m in enumerate(moves)]
    for cp in loads:
        cp.start()
    for one, two in zip(loads, stores):
        one.wait()
        two.start()
    for cp in stores:
        cp.wait()


def deliver(b, c):
    pieces = 4
    hbm = pl.BlockSpec(memory_space=pltpu.HBM)
    dma = pltpu.SemaphoreType.DMA
    return pl.pallas_call(
        functools.partial(pass_on, pieces),
        out_shape=(jax.ShapeDtypeStruct(b.shape, b.dtype), jax.ShapeDtypeStruct(c.shape, c.dtype)),
        in_specs=[hbm, hbm],
        out_specs=(hbm, hbm),
        scratch_shapes=[
            pltpu.VMEM(b.shape, b.dtype),
            pltpu.VMEM(c.shape, c.dtype),
            dma((pieces + 1,)),
            dma((pieces + 1,)),
        ],
        compiler_params=pltpu.CompilerParams(vmem_limit_bytes=60 * 1024 * 1024),
    )(b, c)


def body(dims, tensor, factor_a, factor_c, gram_c):
    ni, nj, nk = dims
    rows, kl, il = tensor.shape
    rank = factor_a.shape[1]
    blocks = min(8, rows // (8 * nk * ni))
    levels = (nj - 1).bit_length()
    jb = rows // blocks
    jx = jb // nk
    jz = jx // ni
    kp = -(-kl // 8) * 8
    hops = (ni - 1).bit_length()
    strip = rank // nj
    f32 = jnp.float32
    dma = pltpu.SemaphoreType.DMA
    vmem = pl.BlockSpec(memory_space=pltpu.VMEM)
    b, c = pl.pallas_call(
        functools.partial(kernel, dims, blocks),
        out_shape=(
            jax.ShapeDtypeStruct((rows, rank), f32),
            jax.ShapeDtypeStruct((kl, rank), f32),
        ),
        in_specs=[pl.BlockSpec(memory_space=pltpu.HBM)] * 4,
        out_specs=(pl.BlockSpec(memory_space=pl.ANY), vmem),
        scratch_shapes=[
            pltpu.VMEM((kl, rows, il), f32),
            pltpu.VMEM((kl, rows, rank), f32),
            pltpu.VMEM((rows, rank), f32),
            pltpu.VMEM((blocks, nk - 1, jx, rank), f32),
            pltpu.VMEM((blocks, jx, rank), f32),
            pltpu.VMEM((blocks, jx, rank), f32),
            pltpu.VMEM((rows, rank), f32),
            pltpu.VMEM((rows, rank), f32),
            pltpu.VMEM((rank, rank), f32),
            pltpu.VMEM((ni, strip, rank), f32),
            pltpu.VMEM((rank, rank), f32),
            pltpu.VMEM((rank, rank), f32),
            pltpu.VMEM((levels, rank // 2, rank), f32),
            pltpu.VMEM((levels, rank // 2, rank), f32),
            pltpu.VMEM((rank, rank), f32),
            pltpu.VMEM((ni * nj, kp, rank), f32),
            pltpu.VMEM((2 * rank, 2 * rank), jnp.bfloat16),
            pltpu.VMEM((2 * rank, rank), jnp.bfloat16),
            pltpu.VMEM((kp, rank), f32),
            pltpu.VMEM((il, rank), f32),
            pltpu.VMEM((kl, rank), f32),
            pltpu.VMEM((rank, rank), f32),
            dma((blocks, kl)),
            dma((blocks, nk - 1)),
            dma((blocks, nk - 1)),
            dma((blocks, hops)),
            dma((blocks, hops)),
            dma((blocks, hops)),
            dma((blocks, hops)),
            dma((blocks, nk - 1)),
            dma((blocks, nk - 1)),
            dma((ni - 1,)),
            dma((ni - 1,)),
            dma((nj - 1,)),
            dma((nj - 1,)),
            dma((levels + 1,)),
            dma((levels + 1,)),
            dma((ni * nj - 1,)),
            dma((ni * nj - 1,)),
            dma((blocks,)),
            dma((3,)),
        ],
        compiler_params=pltpu.CompilerParams(
            collective_id=0, has_side_effects=True, vmem_limit_bytes=60 * 1024 * 1024
        ),
    )(tensor, factor_a, factor_c, gram_c)
    return deliver(b, c)


def solution(mesh):
    dims = (mesh.shape["ia"], mesh.shape["ja"], mesh.shape["ka"])
    placed = (P("ja", "ka", "ia"), P("ia", None), P("ka", None), P())
    return jax.shard_map(
        functools.partial(body, dims),
        mesh=mesh,
        in_specs=placed,
        out_specs=(P("ja", None), P("ka", None)),
        check_vma=False,
    )
```

```python
import functools

import jax
import jax.numpy as jnp
from jax import lax
from jax.experimental import pallas as pl
from jax.experimental.pallas import tpu as pltpu
from jax.sharding import PartitionSpec as P

HIGH = lax.Precision.HIGHEST
MESH = pl.DeviceIdType.MESH
PANEL = 64
WARM, FIRST, BEGIN, X_TIME, HOP = 2.0, 3.7, 3.0, 11.4, 2.5
LAG = (3.2, 3.2, 3.2, 3.2, 0.0)
REDUCE_AT, GRAM_AT, UNIT = 6.3, 9.5, 0.35
PIECE = 8
NB = 16
KL = 56 * 1024 * 1024


def mm(a, b):
    return jnp.dot(a, b, precision=HIGH, preferred_element_type=jnp.float32)


def split3(x):
    a = x.astype(jnp.bfloat16)
    x = x - a.astype(jnp.float32)
    b = x.astype(jnp.bfloat16)
    c = (x - b.astype(jnp.float32)).astype(jnp.bfloat16)
    return a, b, c


def pack_right(w):
    b1, b2, b3 = split3(w)
    top = jnp.concatenate([b1, b2], axis=1)
    return jnp.concatenate([top, top], axis=0), jnp.concatenate([b1, b3], axis=0)


def mm_packed(x, first, second):
    n = second.shape[1]
    a1, a2, a3 = split3(x)
    y = jnp.dot(jnp.concatenate([a1, a2], axis=1), first, preferred_element_type=jnp.float32)
    z = jnp.dot(jnp.concatenate([a3, a1], axis=1), second, preferred_element_type=jnp.float32)
    return y[:, :n] + (y[:, n:] + z)


def mtm(a):
    return lax.dot_general(
        a, a, (((0,), (0,)), ((), ())), precision=HIGH, preferred_element_type=jnp.float32
    )


def take_pivots(rows, q, at):
    n = rows[0].shape[1]
    lane = lax.broadcasted_iota(jnp.int32, (PIECE, n), 1)
    sub = lax.broadcasted_iota(jnp.int32, (PIECE, n), 0)
    lane_row = lax.broadcasted_iota(jnp.int32, (1, n), 1)
    order = [q] + [v for v in range(len(rows)) if v != q]
    cols = {
        v: [jnp.broadcast_to(rows[v][:, at + j : at + j + 1], (PIECE, n)) for j in range(PIECE)]
        for v in order
    }
    x, ahead = rows[q], list(cols[q])
    for t in range(0, PIECE, 2):
        c0, c1 = ahead[t], ahead[t + 1]
        p, r = c0[t : t + 1], c1[t : t + 1]
        u, s = c0[t + 1 : t + 2], c1[t + 1 : t + 2]
        inv = 1.0 / (p * s - r * u)

        def step(y0, y1, kept):
            w0 = (s * y0 - r * y1) * inv
            w1 = (p * y1 - u * y0) * inv
            rest = kept - c0 * w0 - c1 * w1
            return jnp.where(sub == t, w0, jnp.where(sub == t + 1, w1, rest))

        for j in range(t + 2, PIECE):
            y = ahead[j]
            ahead[j] = step(y[t : t + 1], y[t + 1 : t + 2], y)
        here, there = lane_row == at + t, lane_row == at + t + 1
        y0 = jnp.where(here, 1.0, jnp.where(there, 0.0, x[t : t + 1]))
        y1 = jnp.where(here, 0.0, jnp.where(there, 1.0, x[t + 1 : t + 2]))
        x = step(y0, y1, jnp.where((lane == at + t) | (lane == at + t + 1), 0.0, x))
    own = (lane >= at) & (lane < at + PIECE)
    out = list(rows)
    out[q] = x
    for v in order[1:]:
        terms = [cols[v][j] * x[j : j + 1] for j in range(PIECE)]
        while len(terms) > 1:
            terms = [terms[i] + terms[i + 1] for i in range(0, len(terms), 2)]
        out[v] = jnp.where(own, 0.0, rows[v]) - terms[0]
    return out


def inverse_steps(a):
    n = a.shape[0]
    lane = lax.broadcasted_iota(jnp.int32, (n, n), 1)
    sub = lax.broadcasted_iota(jnp.int32, (n, n), 0)
    for base in range(0, n, PANEL):
        rows = [a[base + m : base + m + PIECE] for m in range(0, PANEL, PIECE)]
        for q in range(len(rows)):
            rows = take_pivots(rows, q, base + PIECE * q)
            if q + 1 < len(rows):
                yield None
        pieces = [jnp.zeros((base, n), jnp.float32)] if base else []
        pieces += rows
        if base + PANEL < n:
            pieces.append(jnp.zeros((n - base - PANEL, n), jnp.float32))
        done = jnp.concatenate(pieces, axis=0)
        inside = (lane >= base) & (lane < base + PANEL)
        factor = jnp.where(inside, a, 0.0)
        rest = jnp.where(inside, 0.0, a) - mm_packed(factor, *pack_right(done))
        a = jnp.where((sub >= base) & (sub < base + PANEL), done, rest)
        yield a


def inverse(a):
    for a in inverse_steps(a):
        pass
    return a


def plan(blocks, groups, units):
    pace = X_TIME / blocks
    events = []
    ready = [0.0] * blocks
    per = blocks // groups
    for g in range(groups):
        events.append((WARM + FIRST / groups * (g + 1), g * per, "first", g))
    for b in range(blocks):
        t = BEGIN + pace * (b + 1) + HOP
        for n, name in enumerate(("second", "fold", "third", "center_done", "outer_done")):
            events.append((t, b, name, b))
            ready[b] = t
            t += LAG[n]
    link = BEGIN + X_TIME
    for b in range(blocks):
        link = max(link, ready[b]) + pace
        if b % per == per - 1:
            events.append((link + HOP, b, "fifth", b // per))
    events.append((REDUCE_AT, blocks, "gram_reduce", None))
    for n in range(units):
        events.append((GRAM_AT + n * UNIT, blocks, "side", None))
    return [(name, b) for _, _, name, b in sorted(events, key=lambda e: e[:2])]


def scales(h):
    n = h.shape[0]
    eye = lax.broadcasted_iota(jnp.int32, (n, n), 1) == lax.broadcasted_iota(jnp.int32, (n, n), 0)
    kept = jnp.where(eye, h, 0.0)
    across = lax.rsqrt(jnp.sum(kept, axis=0, keepdims=True))
    down = lax.rsqrt(jnp.sum(kept, axis=1, keepdims=True))
    return down, across


def kernel(
    dims,
    blocks,
    groups,
    t_hbm,
    a_hbm,
    c_hbm,
    gc_hbm,
    b_out,
    c_out,
    tbuf,
    part,
    mloc,
    xrecv,
    xsum,
    zrecv,
    zhalf,
    mfull,
    ga_loc,
    ga_in,
    ga_full,
    g1,
    g_in,
    g_out,
    g3,
    mc_all,
    inv_a,
    inv_b,
    acc_ref,
    a_ref,
    c_ref,
    gc_ref,
    t_sem,
    x_send,
    x_recv,
    z_send,
    z_recv,
    p_send,
    p_recv,
    q_send,
    q_recv,
    ga_send,
    ga_recv,
    gf_send,
    gf_recv,
    g_send,
    g_recv,
    mc_send,
    mc_recv,
    i_sem,
):
    ni, nj, nk = dims
    kl, rows, rank = part.shape
    jb = rows // blocks
    jx = jb // nk
    jg = rows // groups
    per = blocks // groups
    mi, mj, mk = lax.axis_index("ia"), lax.axis_index("ja"), lax.axis_index("ka")
    sends = []

    def peer(axis, me, n, d):
        return {axis: lax.rem(me + d, n)}

    def planned(src, dst, ss, rs, who):
        return pltpu.make_async_remote_copy(
            src_ref=src, dst_ref=dst, send_sem=ss, recv_sem=rs, device_id=who, device_id_type=MESH
        )

    def remote(src, dst, ss, rs, who):
        cp = planned(src, dst, ss, rs, who)
        cp.start()
        sends.append(cp)
        return cp

    icopies = []
    for n, (src, dst) in enumerate(((a_hbm, a_ref), (c_hbm, c_ref), (gc_hbm, gc_ref))):
        cp = pltpu.make_async_copy(src, dst, i_sem.at[n])
        cp.start()
        icopies.append(cp)
    tcopies = {}
    for b in range(groups):
        for k in range(kl):
            rs = pl.ds(b * jg, jg)
            cp = pltpu.make_async_copy(t_hbm.at[rs, k, :], tbuf.at[k, rs, :], t_sem.at[b, k])
            cp.start()
            tcopies[b, k] = cp

    barrier = pltpu.get_barrier_semaphore()
    for d in range(1, ni):
        pl.semaphore_signal(barrier, inc=1, device_id=peer("ia", mi, ni, d), device_id_type=MESH)
    for d in range(1, nj):
        pl.semaphore_signal(barrier, inc=1, device_id=peer("ja", mj, nj, d), device_id_type=MESH)
    for d in range(1, nk):
        pl.semaphore_signal(barrier, inc=1, device_id=peer("ka", mk, nk, d), device_id_type=MESH)

    for cp in icopies:
        cp.wait()
    a = a_ref[...]
    a_hi = a.astype(jnp.bfloat16)
    a_lo = (a - a_hi.astype(jnp.float32)).astype(jnp.bfloat16)
    weights = jnp.concatenate([a_hi, a_lo], axis=1)
    ga_loc[...] = mtm(a)

    x_cp, z_cp, p_cp, q_cp = {}, {}, {}, {}
    step = min(256, jg)

    def first(b):
        for k in range(kl):
            tcopies[b, k].wait()

        def chunk(s, carry):
            rs = pl.ds(pl.multiple_of(b * jg + s * step, step), step)
            total = None
            for k in range(kl):
                x = tbuf[k, rs, :]
                hi = x.astype(jnp.bfloat16)
                lo = (x - hi.astype(jnp.float32)).astype(jnp.bfloat16)
                y = jnp.dot(hi, weights, preferred_element_type=jnp.float32) + jnp.dot(
                    lo, weights, preferred_element_type=jnp.float32
                )
                y = y[:, :rank] + y[:, rank:]
                part[k, rs, :] = y
                y = y * c_ref[k : k + 1, :]
                total = y if total is None else total + y
            mloc[rs, :] = total
            return carry

        lax.fori_loop(0, jg // step, chunk, 0)

    def send_first(g):
        for b in range(g * per, g * per + per):
            for d in range(1, nk):
                other = lax.rem(mk + d, nk)
                rs = pl.ds(pl.multiple_of(b * jb + other * jx, 8), jx)
                x_cp[b, d] = remote(
                    mloc.at[rs, :], xrecv.at[b, d - 1], x_send.at[b, d - 1], x_recv.at[b, d - 1],
                    peer("ka", mk, nk, d),
                )

    def own_rows(b, at, size):
        return pl.ds(pl.multiple_of(b * jb + mk * jx + at, 8), size)

    middle = ni // 2
    low_side = mi < middle
    is_center = (mi == middle - 1) | (mi == middle)
    has_outer = (mi > 0) & (mi < ni - 1)
    inward = {"ia": jnp.clip(jnp.where(low_side, mi + 1, mi - 1), 0, ni - 1)}
    outward = {"ia": jnp.clip(jnp.where(low_side, mi - 1, mi + 1), 0, ni - 1)}
    across = {"ia": ni - 1 - mi}
    jh = jx // 2
    keep = jnp.where(low_side, 0, jh)
    give = jh - keep
    fold_cp, part_cp, half_cp, unfold_cp = {}, {}, {}, {}
    for b in range(blocks):
        fold_cp[b] = planned(
            xsum.at[b], zrecv.at[b], z_send.at[b, 0], z_recv.at[b, 0], inward
        )
        part_cp[b] = planned(
            xsum.at[b, pl.ds(pl.multiple_of(give, 8), jh), :], zhalf.at[b],
            z_send.at[b, 1], z_recv.at[b, 1], across,
        )
        rs = own_rows(b, keep, jh)
        half_cp[b] = planned(
            mfull.at[rs, :], mfull.at[rs, :], p_send.at[b, 0], p_recv.at[b, 0], across
        )
        rs = own_rows(b, 0, jx)
        unfold_cp[b] = planned(
            mfull.at[rs, :], mfull.at[rs, :], p_send.at[b, 1], p_recv.at[b, 1], outward
        )
        for d in range(1, nk):
            q_cp[b, d] = planned(
                mfull.at[rs, :], mfull.at[rs, :], q_send.at[b, d - 1], q_recv.at[b, d - 1],
                peer("ka", mk, nk, d),
            )
            sends.append(q_cp[b, d])

    def second(b):
        total = mloc[own_rows(b, 0, jx), :]
        for d in range(1, nk):
            x_cp[b, d].wait_recv()
            total = total + xrecv[b, d - 1]
        xsum[b] = total

        @pl.when(jnp.logical_not(has_outer))
        def _():
            fold_cp[b].start()

    def fold(b):
        @pl.when(has_outer)
        def _():
            fold_cp[b].wait_recv()
            xsum[b] = xsum[b] + zrecv[b]

            @pl.when(is_center)
            def _():
                part_cp[b].start()

            @pl.when(jnp.logical_not(is_center))
            def _():
                fold_cp[b].start()

    def third(b):
        @pl.when(is_center)
        def _():
            part_cp[b].wait_recv()
            mine = xsum[b, pl.ds(pl.multiple_of(keep, 8), jh), :] + zhalf[b]
            mfull[own_rows(b, keep, jh), :] = mine
            half_cp[b].start()

    def center_done(b):
        @pl.when(is_center)
        def _():
            half_cp[b].wait_recv()
            unfold_cp[b].start()
            for d in range(1, nk):
                q_cp[b, d].start()

    def outer_done(b):
        @pl.when(jnp.logical_not(is_center))
        def _():
            unfold_cp[b].wait_recv()

            @pl.when(has_outer)
            def _():
                unfold_cp[b].start()

            for d in range(1, nk):
                q_cp[b, d].start()

    def settle(b):
        @pl.when(jnp.logical_not(is_center))
        def _():
            fold_cp[b].wait_send()

        @pl.when(is_center)
        def _():
            part_cp[b].wait_send()
            half_cp[b].wait_send()

        @pl.when(has_outer)
        def _():
            unfold_cp[b].wait_send()

    def fifth(g):
        for b in range(g * per, g * per + per):
            for d in range(1, nk):
                q_cp[b, d].wait_recv()
        rs = pl.ds(g * jg, jg)
        value = mm_packed(mfull[rs, :], inv_a[...], inv_b[...])
        b_out[rs, :] = value
        gram = mtm(value)
        g1[...] = gram if g == 0 else g1[...] + gram
        return value

    def sixth(g, value):
        rs = pl.ds(g * jg, jg)
        for k in range(kl):
            s = jnp.sum(part[k, rs, :] * value, axis=0, keepdims=True)
            acc_ref[pl.ds(k, 1), :] = acc_ref[pl.ds(k, 1), :] + s

    ahead = min(2, groups)
    for b in range(ahead):
        first(b)
    pl.semaphore_wait(barrier, ni + nj + nk - 3)
    strip = rank // nj
    part_rows = pl.ds(pl.multiple_of(mj * strip, 8), strip)
    ga_in[mi] = ga_loc[part_rows, :]
    ga_cp = [
        remote(
            ga_loc.at[part_rows, :], ga_in.at[mi], ga_send.at[d - 1], ga_recv.at[d - 1],
            peer("ia", mi, ni, d),
        )
        for d in range(1, ni)
    ]
    for b in range(ahead):
        send_first(b)
    gf_cp = []
    state = {}

    def gram_reduce():
        for cp in ga_cp:
            cp.wait_recv()
        total = ga_in[0]
        for d in range(1, ni):
            total = total + ga_in[d]
        ga_full[part_rows, :] = total
        for d in range(1, nj):
            gf_cp.append(
                remote(
                    ga_full.at[part_rows, :], ga_full.at[part_rows, :], gf_send.at[d - 1],
                    gf_recv.at[d - 1], peer("ja", mj, nj, d),
                )
            )

    def side_steps():
        for cp in gf_cp:
            cp.wait_recv()
        h = ga_full[...] * gc_ref[...]
        down, across = scales(h)
        for h in inverse_steps(h * down * across):
            yield
        inv_a[...], inv_b[...] = pack_right(h * down * across)
        yield

    acc_ref[...] = jnp.zeros_like(acc_ref)
    units = rank // PIECE + 1
    side = side_steps()
    left = units

    def advance(count):
        for _ in range(count):
            next(side)

    stages = {
        "second": second,
        "fold": fold,
        "third": third,
        "center_done": center_done,
        "outer_done": outer_done,
    }
    for name, b in plan(blocks, groups, units):
        if name == "first":
            if b >= ahead:
                first(b)
                send_first(b)
        elif name == "gram_reduce":
            gram_reduce()
        elif name == "side":
            if left:
                advance(1)
                left -= 1
        elif name == "fifth":
            advance(left)
            left = 0
            value = fifth(b)
            if b + 1 < groups:
                sixth(b, value)
        else:
            stages[name](b)

    early = list(sends)
    sends.clear()
    half = rank // 2
    low = lax.rem(mj, 2)
    mine = pl.ds(pl.multiple_of(low * half, 8), half)
    other = pl.ds(pl.multiple_of((1 - low) * half, 8), half)
    partner = {"ja": mj + 1 - 2 * low}
    cp = remote(g1.at[other, :], g_in.at[0], g_send.at[0], g_recv.at[0], partner)
    sixth(groups - 1, value)
    cp.wait_recv()
    total = g1[mine, :] + g_in[0]
    level = 1
    mc_cp = []

    def send_c():
        mc_all[mi * nj + mj] = acc_ref[...]
        for d in range(ni):
            for e in range(nj):
                if d + e:
                    where = {**peer("ia", mi, ni, d), **peer("ja", mj, nj, e)}
                    n = d * nj + e - 1
                    slot = mc_all.at[mi * nj + mj]
                    mc_cp.append(remote(slot, slot, mc_send.at[n], mc_recv.at[n], where))

    while 2**level < nj:
        hop = 2**level
        bit = lax.rem(lax.div(mj, hop), 2)
        g_out[level - 1] = total
        cp = remote(
            g_out.at[level - 1], g_in.at[level], g_send.at[level], g_recv.at[level],
            {"ja": mj + hop * (1 - 2 * bit)},
        )
        if level == 1:
            send_c()
            for b in range(blocks):
                settle(b)
            for one in early:
                one.wait_send()
        cp.wait_recv()
        total = total + g_in[level]
        level += 1
    if level == 1:
        send_c()
        for b in range(blocks):
            settle(b)
        for one in early:
            one.wait_send()
    g3[mine, :] = total
    cp = remote(g3.at[mine, :], g3.at[mine, :], g_send.at[level], g_recv.at[level], partner)
    for one in sends[:-1]:
        one.wait_send()
    sends[:] = sends[-1:]
    cp.wait_recv()
    h = ga_full[...] * g3[...]
    down, across = scales(h)
    h = h * down * across
    first_w, second_w = pack_right(inverse(h) * down * across)
    for cp in mc_cp:
        cp.wait_recv()
    mttkrp_c = mc_all[0]
    for n in range(1, ni * nj):
        mttkrp_c = mttkrp_c + mc_all[n]
    c_out[...] = mm_packed(mttkrp_c, first_w, second_w)[:kl, :]
    for cp in sends:
        cp.wait_send()


def pass_on(b_ref, c_ref, b_out, c_out, sems):
    pairs = ((c_ref, c_out), (b_ref, b_out))
    moves = [pltpu.make_async_copy(src, dst, sems.at[n]) for n, (src, dst) in enumerate(pairs)]
    for cp in moves:
        cp.start()
    for cp in moves:
        cp.wait()


def deliver(b, c):
    hbm = pl.BlockSpec(memory_space=pltpu.HBM)
    vmem = pl.BlockSpec(memory_space=pltpu.VMEM)
    return pl.pallas_call(
        pass_on,
        out_shape=(jax.ShapeDtypeStruct(b.shape, b.dtype), jax.ShapeDtypeStruct(c.shape, c.dtype)),
        in_specs=[vmem, vmem],
        out_specs=(hbm, hbm),
        scratch_shapes=[pltpu.SemaphoreType.DMA((2,))],
        compiler_params=pltpu.CompilerParams(vmem_limit_bytes=4 * 1024 * 1024),
    )(b, c)


def body(dims, tensor, factor_a, factor_c, gram_c):
    ni, nj, nk = dims
    rows, kl, il = tensor.shape
    rank = factor_a.shape[1]
    blocks = min(NB, rows // (16 * nk))
    groups = min(8, blocks)
    levels = (nj - 1).bit_length()
    jb = rows // blocks
    jx = jb // nk
    jg = rows // groups
    per = blocks // groups
    kp = -(-kl // 8) * 8
    strip = rank // nj
    f32 = jnp.float32
    dma = pltpu.SemaphoreType.DMA
    vmem = pl.BlockSpec(memory_space=pltpu.VMEM)
    b, c = pl.pallas_call(
        functools.partial(kernel, dims, blocks, groups),
        out_shape=(pltpu.VMEM((rows, rank), f32), pltpu.VMEM((kl, rank), f32)),
        in_specs=[pl.BlockSpec(memory_space=pltpu.HBM)] * 4,
        out_specs=(vmem, vmem),
        scratch_shapes=[
            pltpu.VMEM((kl, rows, il), f32),
            pltpu.VMEM((kl, rows, rank), f32),
            pltpu.VMEM((rows, rank), f32),
            pltpu.VMEM((blocks, nk - 1, jx, rank), f32),
            pltpu.VMEM((blocks, jx, rank), f32),
            pltpu.VMEM((blocks, jx, rank), f32),
            pltpu.VMEM((blocks, jx // 2, rank), f32),
            pltpu.VMEM((rows, rank), f32),
            pltpu.VMEM((rank, rank), f32),
            pltpu.VMEM((ni, strip, rank), f32),
            pltpu.VMEM((rank, rank), f32),
            pltpu.VMEM((rank, rank), f32),
            pltpu.VMEM((levels, rank // 2, rank), f32),
            pltpu.VMEM((levels, rank // 2, rank), f32),
            pltpu.VMEM((rank, rank), f32),
            pltpu.VMEM((ni * nj, kp, rank), f32),
            pltpu.VMEM((2 * rank, 2 * rank), jnp.bfloat16),
            pltpu.VMEM((2 * rank, rank), jnp.bfloat16),
            pltpu.VMEM((kp, rank), f32),
            pltpu.VMEM((il, rank), f32),
            pltpu.VMEM((kl, rank), f32),
            pltpu.VMEM((rank, rank), f32),
            dma((groups, kl)),
            dma((blocks, nk - 1)),
            dma((blocks, nk - 1)),
            dma((blocks, 2)),
            dma((blocks, 2)),
            dma((blocks, 2)),
            dma((blocks, 2)),
            dma((blocks, nk - 1)),
            dma((blocks, nk - 1)),
            dma((ni - 1,)),
            dma((ni - 1,)),
            dma((nj - 1,)),
            dma((nj - 1,)),
            dma((levels + 1,)),
            dma((levels + 1,)),
            dma((ni * nj - 1,)),
            dma((ni * nj - 1,)),
            dma((3,)),
        ],
        compiler_params=pltpu.CompilerParams(
            collective_id=0, has_side_effects=True, vmem_limit_bytes=KL
        ),
    )(tensor, factor_a, factor_c, gram_c)
    return deliver(b, c)


def solution(mesh):
    dims = (mesh.shape["ia"], mesh.shape["ja"], mesh.shape["ka"])
    placed = (P("ja", "ka", "ia"), P("ia", None), P("ka", None), P())
    return jax.shard_map(
        functools.partial(body, dims),
        mesh=mesh,
        in_specs=placed,
        out_specs=(P("ja", None), P("ka", None)),
        check_vma=False,
    )
```

```python
import functools

import jax
import jax.numpy as jnp
from jax import lax
from jax.experimental import pallas as pl
from jax.experimental.pallas import tpu as pltpu
from jax.sharding import PartitionSpec as P

HIGH = lax.Precision.HIGHEST
MESH = pl.DeviceIdType.MESH
PANEL = 64
WARM, FIRST, BEGIN, X_TIME, HOP = 2.0, 3.7, 3.0, 11.4, 2.5
LAG = (3.2, 3.2, 3.2, 3.2, 0.0)
REDUCE_AT, GRAM_AT, UNIT = 8, 12, 0.35
PIECE = 8
NB = 16
KL = 56 * 1024 * 1024


def mm(a, b):
    return jnp.dot(a, b, precision=HIGH, preferred_element_type=jnp.float32)


def split3(x):
    a = x.astype(jnp.bfloat16)
    x = x - a.astype(jnp.float32)
    b = x.astype(jnp.bfloat16)
    c = (x - b.astype(jnp.float32)).astype(jnp.bfloat16)
    return a, b, c


def pack_right(w):
    b1, b2, b3 = split3(w)
    top = jnp.concatenate([b1, b2], axis=1)
    return jnp.concatenate([top, top], axis=0), jnp.concatenate([b1, b3], axis=0)


def mm_packed(x, first, second):
    n = second.shape[1]
    a1, a2, a3 = split3(x)
    y = jnp.dot(jnp.concatenate([a1, a2], axis=1), first, preferred_element_type=jnp.float32)
    z = jnp.dot(jnp.concatenate([a3, a1], axis=1), second, preferred_element_type=jnp.float32)
    return y[:, :n] + (y[:, n:] + z)


def mtm(a):
    return lax.dot_general(
        a, a, (((0,), (0,)), ((), ())), precision=HIGH, preferred_element_type=jnp.float32
    )


def take_pivots(rows, q, at):
    n = rows[0].shape[1]
    lane = lax.broadcasted_iota(jnp.int32, (PIECE, n), 1)
    sub = lax.broadcasted_iota(jnp.int32, (PIECE, n), 0)
    lane_row = lax.broadcasted_iota(jnp.int32, (1, n), 1)
    order = [q] + [v for v in range(len(rows)) if v != q]
    cols = {
        v: [jnp.broadcast_to(rows[v][:, at + j : at + j + 1], (PIECE, n)) for j in range(PIECE)]
        for v in order
    }
    x, ahead = rows[q], list(cols[q])
    for t in range(0, PIECE, 2):
        c0, c1 = ahead[t], ahead[t + 1]
        p, r = c0[t : t + 1], c1[t : t + 1]
        u, s = c0[t + 1 : t + 2], c1[t + 1 : t + 2]
        inv = 1.0 / (p * s - r * u)

        def step(y0, y1, kept):
            w0 = (s * y0 - r * y1) * inv
            w1 = (p * y1 - u * y0) * inv
            rest = kept - c0 * w0 - c1 * w1
            return jnp.where(sub == t, w0, jnp.where(sub == t + 1, w1, rest))

        for j in range(t + 2, PIECE):
            y = ahead[j]
            ahead[j] = step(y[t : t + 1], y[t + 1 : t + 2], y)
        here, there = lane_row == at + t, lane_row == at + t + 1
        y0 = jnp.where(here, 1.0, jnp.where(there, 0.0, x[t : t + 1]))
        y1 = jnp.where(here, 0.0, jnp.where(there, 1.0, x[t + 1 : t + 2]))
        x = step(y0, y1, jnp.where((lane == at + t) | (lane == at + t + 1), 0.0, x))
    own = (lane >= at) & (lane < at + PIECE)
    out = list(rows)
    out[q] = x
    for v in order[1:]:
        terms = [cols[v][j] * x[j : j + 1] for j in range(PIECE)]
        while len(terms) > 1:
            terms = [terms[i] + terms[i + 1] for i in range(0, len(terms), 2)]
        out[v] = jnp.where(own, 0.0, rows[v]) - terms[0]
    return out


def inverse_steps(a):
    n = a.shape[0]
    lane = lax.broadcasted_iota(jnp.int32, (n, n), 1)
    sub = lax.broadcasted_iota(jnp.int32, (n, n), 0)
    for base in range(0, n, PANEL):
        rows = [a[base + m : base + m + PIECE] for m in range(0, PANEL, PIECE)]
        for q in range(len(rows)):
            rows = take_pivots(rows, q, base + PIECE * q)
            if q + 1 < len(rows):
                yield None
        pieces = [jnp.zeros((base, n), jnp.float32)] if base else []
        pieces += rows
        if base + PANEL < n:
            pieces.append(jnp.zeros((n - base - PANEL, n), jnp.float32))
        done = jnp.concatenate(pieces, axis=0)
        inside = (lane >= base) & (lane < base + PANEL)
        factor = jnp.where(inside, a, 0.0)
        rest = jnp.where(inside, 0.0, a) - mm_packed(factor, *pack_right(done))
        a = jnp.where((sub >= base) & (sub < base + PANEL), done, rest)
        yield a


def inverse(a):
    for a in inverse_steps(a):
        pass
    return a


def plan(blocks, groups, units):
    pace = X_TIME / blocks
    events = []
    ready = [0.0] * blocks
    per = blocks // groups
    for g in range(groups):
        events.append((WARM + FIRST / groups * (g + 1), g * per, "first", g))
    for b in range(blocks):
        t = BEGIN + pace * (b + 1) + HOP
        for n, name in enumerate(("second", "fold", "third", "center_done", "outer_done")):
            events.append((t, b, name, b))
            ready[b] = t
            t += LAG[n]
    link = BEGIN + X_TIME
    for b in range(blocks):
        link = max(link, ready[b]) + pace
        if b % per == per - 1:
            events.append((link + HOP, b, "fifth", b // per))
    events.append((REDUCE_AT, blocks, "gram_reduce", None))
    for n in range(units):
        events.append((GRAM_AT + n * UNIT, blocks, "side", None))
    return [(name, b) for _, _, name, b in sorted(events, key=lambda e: e[:2])]


def scales(h):
    n = h.shape[0]
    eye = lax.broadcasted_iota(jnp.int32, (n, n), 1) == lax.broadcasted_iota(jnp.int32, (n, n), 0)
    kept = jnp.where(eye, h, 0.0)
    across = lax.rsqrt(jnp.sum(kept, axis=0, keepdims=True))
    down = lax.rsqrt(jnp.sum(kept, axis=1, keepdims=True))
    return down, across


def kernel(
    dims,
    blocks,
    groups,
    t_hbm,
    a_hbm,
    c_hbm,
    gc_hbm,
    b_out,
    c_out,
    tbuf,
    part,
    mloc,
    xrecv,
    xsum,
    zrecv,
    zhalf,
    mfull,
    ga_loc,
    ga_in,
    ga_full,
    g1,
    g_in,
    g_out,
    g3,
    mc_all,
    inv_a,
    inv_b,
    acc_ref,
    a_ref,
    c_ref,
    gc_ref,
    t_sem,
    x_send,
    x_recv,
    z_send,
    z_recv,
    p_send,
    q_send,
    q_recv,
    ga_send,
    ga_recv,
    gf_send,
    gf_recv,
    g_send,
    g_recv,
    mc_send,
    mc_recv,
    i_sem,
):
    ni, nj, nk = dims
    kl, rows, rank = part.shape
    jb = rows // blocks
    jx = jb // nk
    jg = rows // groups
    per = blocks // groups
    mi, mj, mk = lax.axis_index("ia"), lax.axis_index("ja"), lax.axis_index("ka")

    def peer(axis, me, n, d):
        return {axis: lax.rem(me + d, n)}

    def planned(src, dst, ss, rs, who):
        return pltpu.make_async_remote_copy(
            src_ref=src, dst_ref=dst, send_sem=ss, recv_sem=rs, device_id=who, device_id_type=MESH
        )

    def remote(src, dst, ss, rs, who):
        cp = planned(src, dst, ss, rs, who)
        cp.start()
        return cp

    def drained(ref, sem):
        planned(ref, ref, sem, sem, {"ka": mk}).wait_send()

    def landed(ref, sem):
        planned(ref, ref, sem, sem, {"ka": mk}).wait_recv()

    icopies = []
    for n, (src, dst) in enumerate(((a_hbm, a_ref), (c_hbm, c_ref), (gc_hbm, gc_ref))):
        cp = pltpu.make_async_copy(src, dst, i_sem.at[n])
        cp.start()
        icopies.append(cp)
    for b in range(groups):
        for k in range(kl):
            rs = pl.ds(b * jg, jg)
            cp = pltpu.make_async_copy(t_hbm.at[rs, k, :], tbuf.at[k, rs, :], t_sem.at[b])
            cp.start()

    barrier = pltpu.get_barrier_semaphore()
    for d in range(1, ni):
        pl.semaphore_signal(barrier, inc=1, device_id=peer("ia", mi, ni, d), device_id_type=MESH)
    for d in range(1, nj):
        pl.semaphore_signal(barrier, inc=1, device_id=peer("ja", mj, nj, d), device_id_type=MESH)
    for d in range(1, nk):
        pl.semaphore_signal(barrier, inc=1, device_id=peer("ka", mk, nk, d), device_id_type=MESH)

    for cp in icopies:
        cp.wait()
    a = a_ref[...]
    a_hi = a.astype(jnp.bfloat16)
    a_lo = (a - a_hi.astype(jnp.float32)).astype(jnp.bfloat16)
    weights = jnp.concatenate([a_hi, a_lo], axis=1)
    ga_loc[...] = mtm(a)

    x_cp, z_cp, p_cp, q_cp = {}, {}, {}, {}
    step = min(256, jg)

    def first(b):
        piece = tbuf.at[:, pl.ds(b * jg, jg), :]
        pltpu.make_async_copy(piece, piece, t_sem.at[b]).wait()

        def chunk(s, carry):
            rs = pl.ds(pl.multiple_of(b * jg + s * step, step), step)
            total = None
            for k in range(kl):
                x = tbuf[k, rs, :]
                hi = x.astype(jnp.bfloat16)
                lo = (x - hi.astype(jnp.float32)).astype(jnp.bfloat16)
                y = jnp.dot(hi, weights, preferred_element_type=jnp.float32) + jnp.dot(
                    lo, weights, preferred_element_type=jnp.float32
                )
                y = y[:, :rank] + y[:, rank:]
                part[k, rs, :] = y
                y = y * c_ref[k : k + 1, :]
                total = y if total is None else total + y
            mloc[rs, :] = total
            return carry

        lax.fori_loop(0, jg // step, chunk, 0)

    def send_first(g):
        for b in range(g * per, g * per + per):
            for d in range(1, nk):
                other = lax.rem(mk + d, nk)
                rs = pl.ds(pl.multiple_of(b * jb + other * jx, 8), jx)
                x_cp[b, d] = remote(
                    mloc.at[rs, :], xrecv.at[b, d - 1], x_send, x_recv.at[b, d - 1],
                    peer("ka", mk, nk, d),
                )

    def own_rows(b, at, size):
        return pl.ds(pl.multiple_of(b * jb + mk * jx + at, 8), size)

    middle = ni // 2
    low_side = mi < middle
    is_center = (mi == middle - 1) | (mi == middle)
    has_outer = (mi > 0) & (mi < ni - 1)
    inward = {"ia": jnp.clip(jnp.where(low_side, mi + 1, mi - 1), 0, ni - 1)}
    outward = {"ia": jnp.clip(jnp.where(low_side, mi - 1, mi + 1), 0, ni - 1)}
    across = {"ia": ni - 1 - mi}
    jh = jx // 2
    keep = jnp.where(low_side, 0, jh)
    give = jh - keep
    fold_cp, part_cp, half_cp, unfold_cp = {}, {}, {}, {}
    for b in range(blocks):
        fold_cp[b] = planned(
            xsum.at[b], zrecv.at[b], z_send.at[0], z_recv.at[b, 0], inward
        )
        part_cp[b] = planned(
            xsum.at[b, pl.ds(pl.multiple_of(give, 8), jh), :], zhalf.at[b],
            z_send.at[1], z_recv.at[b, 1], across,
        )
        rs = own_rows(b, keep, jh)
        half_cp[b] = planned(
            mfull.at[rs, :], mfull.at[rs, :], p_send.at[0], z_recv.at[b, 0], across
        )
        rs = own_rows(b, 0, jx)
        unfold_cp[b] = planned(
            mfull.at[rs, :], mfull.at[rs, :], p_send.at[1], x_recv.at[b, 0], outward
        )
        for d in range(1, nk):
            q_cp[b, d] = planned(
                mfull.at[rs, :], mfull.at[rs, :], q_send, q_recv.at[b // per, d - 1],
                peer("ka", mk, nk, d),
            )

    def second(b):
        total = mloc[own_rows(b, 0, jx), :]
        for d in range(1, nk):
            x_cp[b, d].wait_recv()
            total = total + xrecv[b, d - 1]
        xsum[b] = total

        @pl.when(jnp.logical_not(has_outer))
        def _():
            fold_cp[b].start()

    def fold(b):
        @pl.when(has_outer)
        def _():
            fold_cp[b].wait_recv()
            xsum[b] = xsum[b] + zrecv[b]

            @pl.when(is_center)
            def _():
                part_cp[b].start()

            @pl.when(jnp.logical_not(is_center))
            def _():
                fold_cp[b].start()

    def third(b):
        @pl.when(is_center)
        def _():
            part_cp[b].wait_recv()
            mine = xsum[b, pl.ds(pl.multiple_of(keep, 8), jh), :] + zhalf[b]
            mfull[own_rows(b, keep, jh), :] = mine
            half_cp[b].start()

    def center_done(b):
        @pl.when(is_center)
        def _():
            half_cp[b].wait_recv()
            unfold_cp[b].start()
            for d in range(1, nk):
                q_cp[b, d].start()

    def outer_done(b):
        @pl.when(jnp.logical_not(is_center))
        def _():
            unfold_cp[b].wait_recv()

            @pl.when(has_outer)
            def _():
                unfold_cp[b].start()

            for d in range(1, nk):
                q_cp[b, d].start()

    def settle():
        drained(xrecv, x_send)
        drained(xrecv, q_send)
        drained(ga_in.at[pl.ds(0, ni - 1)], ga_send)
        drained(ga_full.at[pl.ds(0, (nj - 1) * strip), :], gf_send)

        @pl.when(jnp.logical_not(is_center))
        def _():
            drained(zrecv, z_send.at[0])

        @pl.when(is_center)
        def _():
            drained(zhalf, z_send.at[1])
            drained(zhalf, p_send.at[0])

        @pl.when(has_outer)
        def _():
            drained(zrecv, p_send.at[1])

    def fifth(g):
        for d in range(1, nk):
            landed(mfull.at[pl.ds(0, per * jx), :], q_recv.at[g, d - 1])
        rs = pl.ds(g * jg, jg)
        value = mm_packed(mfull[rs, :], inv_a[...], inv_b[...])
        b_out[rs, :] = value
        gram = mtm(value)
        g1[...] = gram if g == 0 else g1[...] + gram
        return value

    def sixth(g, value):
        rs = pl.ds(g * jg, jg)
        for k in range(kl):
            s = jnp.sum(part[k, rs, :] * value, axis=0, keepdims=True)
            acc_ref[pl.ds(k, 1), :] = acc_ref[pl.ds(k, 1), :] + s

    ahead = min(2, groups)
    for b in range(ahead):
        first(b)
    pl.semaphore_wait(barrier, ni + nj + nk - 3)
    strip = rank // nj
    part_rows = pl.ds(pl.multiple_of(mj * strip, 8), strip)
    ga_in[mi] = ga_loc[part_rows, :]
    for d in range(1, ni):
        remote(
            ga_loc.at[part_rows, :], ga_in.at[mi], ga_send, ga_recv, peer("ia", mi, ni, d)
        )
    for b in range(ahead):
        send_first(b)
    state = {}

    def gram_reduce():
        landed(ga_in.at[pl.ds(0, ni - 1)], ga_recv)
        total = ga_in[0]
        for d in range(1, ni):
            total = total + ga_in[d]
        ga_full[part_rows, :] = total
        for d in range(1, nj):
            rows_here = ga_full.at[part_rows, :]
            remote(rows_here, rows_here, gf_send, gf_recv, peer("ja", mj, nj, d))

    def side_steps():
        landed(ga_full.at[pl.ds(0, (nj - 1) * strip), :], gf_recv)
        h = ga_full[...] * gc_ref[...]
        down, across = scales(h)
        for h in inverse_steps(h * down * across):
            yield
        inv_a[...], inv_b[...] = pack_right(h * down * across)
        yield

    acc_ref[...] = jnp.zeros_like(acc_ref)
    units = rank // PIECE + 1
    side = side_steps()
    left = units

    def advance(count):
        for _ in range(count):
            next(side)

    stages = {
        "second": second,
        "fold": fold,
        "third": third,
        "center_done": center_done,
        "outer_done": outer_done,
    }
    for name, b in plan(blocks, groups, units):
        if name == "first":
            if b >= ahead:
                first(b)
                send_first(b)
        elif name == "gram_reduce":
            gram_reduce()
        elif name == "side":
            if left:
                advance(1)
                left -= 1
        elif name == "fifth":
            advance(left)
            left = 0
            value = fifth(b)
            if b + 1 < groups:
                sixth(b, value)
        else:
            stages[name](b)

    half = rank // 2
    low = lax.rem(mj, 2)
    mine = pl.ds(pl.multiple_of(low * half, 8), half)
    other = pl.ds(pl.multiple_of((1 - low) * half, 8), half)
    partner = {"ja": mj + 1 - 2 * low}
    cp = remote(g1.at[other, :], g_in.at[0], g_send.at[0], g_recv.at[0], partner)
    hops = [cp]
    sixth(groups - 1, value)
    cp.wait_recv()
    total = g1[mine, :] + g_in[0]
    level = 1

    def send_c():
        mc_all[mi * nj + mj] = acc_ref[...]
        for d in range(ni):
            for e in range(nj):
                if d + e:
                    where = {**peer("ia", mi, ni, d), **peer("ja", mj, nj, e)}
                    slot = mc_all.at[mi * nj + mj]
                    remote(slot, slot, mc_send, mc_recv, where)

    while 2**level < nj:
        hop = 2**level
        bit = lax.rem(lax.div(mj, hop), 2)
        g_out[level - 1] = total
        cp = remote(
            g_out.at[level - 1], g_in.at[level], g_send.at[level], g_recv.at[level],
            {"ja": mj + hop * (1 - 2 * bit)},
        )
        hops.append(cp)
        if level == 1:
            send_c()
            settle()
        cp.wait_recv()
        total = total + g_in[level]
        level += 1
    if level == 1:
        send_c()
        settle()
    g3[mine, :] = total
    cp = remote(g3.at[mine, :], g3.at[mine, :], g_send.at[level], g_recv.at[level], partner)
    others = mc_all.at[pl.ds(0, ni * nj - 1)]
    drained(others, mc_send)
    for one in hops:
        one.wait_send()
    cp.wait_recv()
    h = ga_full[...] * g3[...]
    down, across = scales(h)
    h = h * down * across
    first_w, second_w = pack_right(inverse(h) * down * across)
    landed(others, mc_recv)
    mttkrp_c = mc_all[0]
    for n in range(1, ni * nj):
        mttkrp_c = mttkrp_c + mc_all[n]
    c_out[...] = mm_packed(mttkrp_c, first_w, second_w)[:kl, :]
    cp.wait_send()


def pass_on(b_ref, c_ref, b_out, c_out, sems):
    pairs = ((c_ref, c_out), (b_ref, b_out))
    moves = [pltpu.make_async_copy(src, dst, sems.at[n]) for n, (src, dst) in enumerate(pairs)]
    for cp in moves:
        cp.start()
    for cp in moves:
        cp.wait()


def deliver(b, c):
    hbm = pl.BlockSpec(memory_space=pltpu.HBM)
    vmem = pl.BlockSpec(memory_space=pltpu.VMEM)
    return pl.pallas_call(
        pass_on,
        out_shape=(jax.ShapeDtypeStruct(b.shape, b.dtype), jax.ShapeDtypeStruct(c.shape, c.dtype)),
        in_specs=[vmem, vmem],
        out_specs=(hbm, hbm),
        scratch_shapes=[pltpu.SemaphoreType.DMA((2,))],
        compiler_params=pltpu.CompilerParams(vmem_limit_bytes=4 * 1024 * 1024),
    )(b, c)


def body(dims, tensor, factor_a, factor_c, gram_c):
    ni, nj, nk = dims
    rows, kl, il = tensor.shape
    rank = factor_a.shape[1]
    blocks = min(NB, rows // (16 * nk))
    groups = min(8, blocks)
    levels = (nj - 1).bit_length()
    jb = rows // blocks
    jx = jb // nk
    jg = rows // groups
    per = blocks // groups
    kp = -(-kl // 8) * 8
    strip = rank // nj
    f32 = jnp.float32
    dma = pltpu.SemaphoreType.DMA
    vmem = pl.BlockSpec(memory_space=pltpu.VMEM)
    b, c = pl.pallas_call(
        functools.partial(kernel, dims, blocks, groups),
        out_shape=(pltpu.VMEM((rows, rank), f32), pltpu.VMEM((kl, rank), f32)),
        in_specs=[pl.BlockSpec(memory_space=pltpu.HBM)] * 4,
        out_specs=(vmem, vmem),
        scratch_shapes=[
            pltpu.VMEM((kl, rows, il), f32),
            pltpu.VMEM((kl, rows, rank), f32),
            pltpu.VMEM((rows, rank), f32),
            pltpu.VMEM((blocks, nk - 1, jx, rank), f32),
            pltpu.VMEM((blocks, jx, rank), f32),
            pltpu.VMEM((blocks, jx, rank), f32),
            pltpu.VMEM((blocks, jx // 2, rank), f32),
            pltpu.VMEM((rows, rank), f32),
            pltpu.VMEM((rank, rank), f32),
            pltpu.VMEM((ni, strip, rank), f32),
            pltpu.VMEM((rank, rank), f32),
            pltpu.VMEM((rank, rank), f32),
            pltpu.VMEM((levels, rank // 2, rank), f32),
            pltpu.VMEM((levels, rank // 2, rank), f32),
            pltpu.VMEM((rank, rank), f32),
            pltpu.VMEM((ni * nj, kp, rank), f32),
            pltpu.VMEM((2 * rank, 2 * rank), jnp.bfloat16),
            pltpu.VMEM((2 * rank, rank), jnp.bfloat16),
            pltpu.VMEM((kp, rank), f32),
            pltpu.VMEM((il, rank), f32),
            pltpu.VMEM((kl, rank), f32),
            pltpu.VMEM((rank, rank), f32),
            dma((groups,)),
            dma,
            dma((blocks, nk - 1)),
            dma((2,)),
            dma((blocks, 2)),
            dma((2,)),
            dma,
            dma((groups, nk - 1)),
            dma,
            dma,
            dma,
            dma,
            dma((levels + 1,)),
            dma((levels + 1,)),
            dma,
            dma,
            dma((3,)),
        ],
        compiler_params=pltpu.CompilerParams(
            collective_id=0, has_side_effects=True, vmem_limit_bytes=KL
        ),
    )(tensor, factor_a, factor_c, gram_c)
    return deliver(b, c)


def solution(mesh):
    dims = (mesh.shape["ia"], mesh.shape["ja"], mesh.shape["ka"])
    placed = (P("ja", "ka", "ia"), P("ia", None), P("ka", None), P())
    return jax.shard_map(
        functools.partial(body, dims),
        mesh=mesh,
        in_specs=placed,
        out_specs=(P("ja", None), P("ka", None)),
        check_vma=False,
    )
```

```python
import functools

import jax
import jax.numpy as jnp
from jax import lax
from jax.experimental import pallas as pl
from jax.experimental.pallas import tpu as pltpu
from jax.sharding import PartitionSpec as P

HIGH = lax.Precision.HIGHEST
MESH = pl.DeviceIdType.MESH
PANEL = 64
WARM, FIRST, BEGIN, X_TIME, HOP = 2.0, 3.7, 3.0, 11.4, 2.5
LAG = (3.2, 3.2, 3.2, 3.2, 0.0)
REDUCE_AT, GRAM_AT, UNIT = 8, 12, 0.35
PIECE = 8
NB = 16
LEG = 4.0
KL = 56 * 1024 * 1024


def mm(a, b):
    return jnp.dot(a, b, precision=HIGH, preferred_element_type=jnp.float32)


def split3(x):
    a = x.astype(jnp.bfloat16)
    x = x - a.astype(jnp.float32)
    b = x.astype(jnp.bfloat16)
    c = (x - b.astype(jnp.float32)).astype(jnp.bfloat16)
    return a, b, c


def pack_right(w):
    b1, b2, b3 = split3(w)
    top = jnp.concatenate([b1, b2], axis=1)
    return jnp.concatenate([top, top], axis=0), jnp.concatenate([b1, b3], axis=0)


def mm_packed(x, first, second):
    n = second.shape[1]
    a1, a2, a3 = split3(x)
    y = jnp.dot(jnp.concatenate([a1, a2], axis=1), first, preferred_element_type=jnp.float32)
    z = jnp.dot(jnp.concatenate([a3, a1], axis=1), second, preferred_element_type=jnp.float32)
    return y[:, :n] + (y[:, n:] + z)


def mtm(a):
    return lax.dot_general(
        a, a, (((0,), (0,)), ((), ())), precision=HIGH, preferred_element_type=jnp.float32
    )


def take_pivots(rows, q, at):
    n = rows[0].shape[1]
    lane = lax.broadcasted_iota(jnp.int32, (PIECE, n), 1)
    sub = lax.broadcasted_iota(jnp.int32, (PIECE, n), 0)
    lane_row = lax.broadcasted_iota(jnp.int32, (1, n), 1)
    order = [q] + [v for v in range(len(rows)) if v != q]
    cols = {
        v: [jnp.broadcast_to(rows[v][:, at + j : at + j + 1], (PIECE, n)) for j in range(PIECE)]
        for v in order
    }
    x, ahead = rows[q], list(cols[q])
    for t in range(0, PIECE, 2):
        c0, c1 = ahead[t], ahead[t + 1]
        p, r = c0[t : t + 1], c1[t : t + 1]
        u, s = c0[t + 1 : t + 2], c1[t + 1 : t + 2]
        inv = 1.0 / (p * s - r * u)

        def step(y0, y1, kept):
            w0 = (s * y0 - r * y1) * inv
            w1 = (p * y1 - u * y0) * inv
            rest = kept - c0 * w0 - c1 * w1
            return jnp.where(sub == t, w0, jnp.where(sub == t + 1, w1, rest))

        for j in range(t + 2, PIECE):
            y = ahead[j]
            ahead[j] = step(y[t : t + 1], y[t + 1 : t + 2], y)
        here, there = lane_row == at + t, lane_row == at + t + 1
        y0 = jnp.where(here, 1.0, jnp.where(there, 0.0, x[t : t + 1]))
        y1 = jnp.where(here, 0.0, jnp.where(there, 1.0, x[t + 1 : t + 2]))
        x = step(y0, y1, jnp.where((lane == at + t) | (lane == at + t + 1), 0.0, x))
    own = (lane >= at) & (lane < at + PIECE)
    out = list(rows)
    out[q] = x
    for v in order[1:]:
        terms = [cols[v][j] * x[j : j + 1] for j in range(PIECE)]
        while len(terms) > 1:
            terms = [terms[i] + terms[i + 1] for i in range(0, len(terms), 2)]
        out[v] = jnp.where(own, 0.0, rows[v]) - terms[0]
    return out


def inverse_steps(a):
    n = a.shape[0]
    lane = lax.broadcasted_iota(jnp.int32, (n, n), 1)
    sub = lax.broadcasted_iota(jnp.int32, (n, n), 0)
    for base in range(0, n, PANEL):
        rows = [a[base + m : base + m + PIECE] for m in range(0, PANEL, PIECE)]
        for q in range(len(rows)):
            rows = take_pivots(rows, q, base + PIECE * q)
            if q + 1 < len(rows):
                yield None
        pieces = [jnp.zeros((base, n), jnp.float32)] if base else []
        pieces += rows
        if base + PANEL < n:
            pieces.append(jnp.zeros((n - base - PANEL, n), jnp.float32))
        done = jnp.concatenate(pieces, axis=0)
        inside = (lane >= base) & (lane < base + PANEL)
        factor = jnp.where(inside, a, 0.0)
        rest = jnp.where(inside, 0.0, a) - mm_packed(factor, *pack_right(done))
        a = jnp.where((sub >= base) & (sub < base + PANEL), done, rest)
        yield a


def inverse(a):
    for a in inverse_steps(a):
        pass
    return a


def plan(blocks, groups, units, legs):
    quarter = max(1, blocks // 4)
    pace = X_TIME / blocks
    events = []
    ready = [0.0] * blocks
    per = blocks // groups
    for g in range(groups):
        events.append((WARM + FIRST / groups * (g + 1), g * per, "first", g))
    for b in range(blocks):
        t = BEGIN + pace * (b + 1) + HOP
        for n, name in enumerate(("second", "fold", "third", "center_done", "outer_done")):
            events.append((t, b, name, b))
            ready[b] = t
            if name == "third" and b % quarter == quarter - 1:
                events.append((max(t, GRAM_AT + units * UNIT) + 0.1, blocks, "own_gram", b // quarter))
                last = events[-1][0]
            t += LAG[n]
    link = BEGIN + X_TIME
    for b in range(blocks):
        link = max(link, ready[b]) + pace
        if b % per == per - 1:
            events.append((link + HOP, b, "fifth", b // per))
    for n in range(legs):
        events.append((last + 0.1 + LEG * n, blocks, "leg", n))
    events.append((REDUCE_AT, blocks, "gram_reduce", None))
    for n in range(units):
        events.append((GRAM_AT + n * UNIT, blocks, "side", None))
    return [(name, b) for _, _, name, b in sorted(events, key=lambda e: e[:2])]


def scales(h):
    n = h.shape[0]
    eye = lax.broadcasted_iota(jnp.int32, (n, n), 1) == lax.broadcasted_iota(jnp.int32, (n, n), 0)
    kept = jnp.where(eye, h, 0.0)
    across = lax.rsqrt(jnp.sum(kept, axis=0, keepdims=True))
    down = lax.rsqrt(jnp.sum(kept, axis=1, keepdims=True))
    return down, across


def kernel(
    dims,
    blocks,
    groups,
    t_hbm,
    a_hbm,
    c_hbm,
    gc_hbm,
    b_out,
    c_out,
    tbuf,
    part,
    mloc,
    xrecv,
    xsum,
    zrecv,
    zhalf,
    mfull,
    ga_loc,
    ga_in,
    ga_full,
    g1,
    g_in,
    g3,
    mc_all,
    inv_a,
    inv_b,
    acc_ref,
    a_ref,
    c_ref,
    gc_ref,
    t_sem,
    x_send,
    x_recv,
    z_send,
    z_recv,
    p_send,
    q_send,
    q_recv,
    ga_send,
    ga_recv,
    gf_send,
    gf_recv,
    g_send,
    g_recv,
    mc_send,
    mc_recv,
    i_sem,
):
    ni, nj, nk = dims
    kl, rows, rank = part.shape
    jb = rows // blocks
    jx = jb // nk
    jg = rows // groups
    per = blocks // groups
    mi, mj, mk = lax.axis_index("ia"), lax.axis_index("ja"), lax.axis_index("ka")

    def peer(axis, me, n, d):
        return {axis: lax.rem(me + d, n)}

    def planned(src, dst, ss, rs, who):
        return pltpu.make_async_remote_copy(
            src_ref=src, dst_ref=dst, send_sem=ss, recv_sem=rs, device_id=who, device_id_type=MESH
        )

    def remote(src, dst, ss, rs, who):
        cp = planned(src, dst, ss, rs, who)
        cp.start()
        return cp

    def drained(ref, sem):
        planned(ref, ref, sem, sem, {"ka": mk}).wait_send()

    def landed(ref, sem):
        planned(ref, ref, sem, sem, {"ka": mk}).wait_recv()

    icopies = []
    for n, (src, dst) in enumerate(((a_hbm, a_ref), (c_hbm, c_ref), (gc_hbm, gc_ref))):
        cp = pltpu.make_async_copy(src, dst, i_sem.at[n])
        cp.start()
        icopies.append(cp)
    for b in range(groups):
        for k in range(kl):
            rs = pl.ds(b * jg, jg)
            cp = pltpu.make_async_copy(t_hbm.at[rs, k, :], tbuf.at[k, rs, :], t_sem.at[b])
            cp.start()

    barrier = pltpu.get_barrier_semaphore()
    for d in range(1, ni):
        pl.semaphore_signal(barrier, inc=1, device_id=peer("ia", mi, ni, d), device_id_type=MESH)
    for d in range(1, nj):
        pl.semaphore_signal(barrier, inc=1, device_id=peer("ja", mj, nj, d), device_id_type=MESH)
    for d in range(1, nk):
        pl.semaphore_signal(barrier, inc=1, device_id=peer("ka", mk, nk, d), device_id_type=MESH)

    for cp in icopies:
        cp.wait()
    a = a_ref[...]
    a_hi = a.astype(jnp.bfloat16)
    a_lo = (a - a_hi.astype(jnp.float32)).astype(jnp.bfloat16)
    weights = jnp.concatenate([a_hi, a_lo], axis=1)
    ga_loc[...] = mtm(a)

    x_cp, z_cp, p_cp, q_cp = {}, {}, {}, {}
    step = min(256, jg)

    def first(b):
        piece = tbuf.at[:, pl.ds(b * jg, jg), :]
        pltpu.make_async_copy(piece, piece, t_sem.at[b]).wait()

        def chunk(s, carry):
            rs = pl.ds(pl.multiple_of(b * jg + s * step, step), step)
            total = None
            for k in range(kl):
                x = tbuf[k, rs, :]
                hi = x.astype(jnp.bfloat16)
                lo = (x - hi.astype(jnp.float32)).astype(jnp.bfloat16)
                y = jnp.dot(hi, weights, preferred_element_type=jnp.float32) + jnp.dot(
                    lo, weights, preferred_element_type=jnp.float32
                )
                y = y[:, :rank] + y[:, rank:]
                part[k, rs, :] = y
                y = y * c_ref[k : k + 1, :]
                total = y if total is None else total + y
            mloc[rs, :] = total
            return carry

        lax.fori_loop(0, jg // step, chunk, 0)

    def send_first(g):
        for b in range(g * per, g * per + per):
            for d in range(1, nk):
                other = lax.rem(mk + d, nk)
                rs = pl.ds(pl.multiple_of(b * jb + other * jx, 8), jx)
                x_cp[b, d] = remote(
                    mloc.at[rs, :], xrecv.at[b, d - 1], x_send, x_recv.at[b, d - 1],
                    peer("ka", mk, nk, d),
                )

    def own_rows(b, at, size):
        return pl.ds(pl.multiple_of(b * jb + mk * jx + at, 8), size)

    middle = ni // 2
    low_side = mi < middle
    is_center = (mi == middle - 1) | (mi == middle)
    has_outer = (mi > 0) & (mi < ni - 1)
    inward = {"ia": jnp.clip(jnp.where(low_side, mi + 1, mi - 1), 0, ni - 1)}
    outward = {"ia": jnp.clip(jnp.where(low_side, mi - 1, mi + 1), 0, ni - 1)}
    across = {"ia": ni - 1 - mi}
    jh = jx // 2
    keep = jnp.where(low_side, 0, jh)
    give = jh - keep
    fold_cp, part_cp, half_cp, unfold_cp = {}, {}, {}, {}
    for b in range(blocks):
        fold_cp[b] = planned(
            xsum.at[b], zrecv.at[b], z_send.at[0], z_recv.at[b, 0], inward
        )
        part_cp[b] = planned(
            xsum.at[b, pl.ds(pl.multiple_of(give, 8), jh), :], zhalf.at[b],
            z_send.at[1], z_recv.at[b, 1], across,
        )
        rs = own_rows(b, keep, jh)
        half_cp[b] = planned(
            mfull.at[rs, :], mfull.at[rs, :], p_send.at[0], z_recv.at[b, 0], across
        )
        rs = own_rows(b, 0, jx)
        unfold_cp[b] = planned(
            mfull.at[rs, :], mfull.at[rs, :], p_send.at[1], x_recv.at[b, 0], outward
        )
        for d in range(1, nk):
            q_cp[b, d] = planned(
                mfull.at[rs, :], mfull.at[rs, :], q_send, q_recv.at[b // per, d - 1],
                peer("ka", mk, nk, d),
            )

    def second(b):
        total = mloc[own_rows(b, 0, jx), :]
        for d in range(1, nk):
            x_cp[b, d].wait_recv()
            total = total + xrecv[b, d - 1]
        xsum[b] = total

        @pl.when(jnp.logical_not(has_outer))
        def _():
            fold_cp[b].start()

    def fold(b):
        @pl.when(has_outer)
        def _():
            fold_cp[b].wait_recv()
            xsum[b] = xsum[b] + zrecv[b]

            @pl.when(is_center)
            def _():
                part_cp[b].start()

            @pl.when(jnp.logical_not(is_center))
            def _():
                fold_cp[b].start()

    def third(b):
        @pl.when(is_center)
        def _():
            part_cp[b].wait_recv()
            mine = xsum[b, pl.ds(pl.multiple_of(keep, 8), jh), :] + zhalf[b]
            mfull[own_rows(b, keep, jh), :] = mine
            half_cp[b].start()

    def center_done(b):
        @pl.when(is_center)
        def _():
            half_cp[b].wait_recv()
            unfold_cp[b].start()
            for d in range(1, nk):
                q_cp[b, d].start()

    def outer_done(b):
        @pl.when(jnp.logical_not(is_center))
        def _():
            unfold_cp[b].wait_recv()

            @pl.when(has_outer)
            def _():
                unfold_cp[b].start()

            for d in range(1, nk):
                q_cp[b, d].start()

    def settle():
        drained(xrecv, x_send)
        drained(xrecv, q_send)
        drained(ga_in.at[pl.ds(0, ni - 1)], ga_send)
        drained(ga_full.at[pl.ds(0, (nj - 1) * strip), :], gf_send)

        @pl.when(jnp.logical_not(is_center))
        def _():
            drained(zrecv, z_send.at[0])

        @pl.when(is_center)
        def _():
            drained(zhalf, z_send.at[1])
            drained(zhalf, p_send.at[0])

        @pl.when(has_outer)
        def _():
            drained(zrecv, p_send.at[1])

    def fifth(g):
        for d in range(1, nk):
            landed(mfull.at[pl.ds(0, per * jx), :], q_recv.at[g, d - 1])
        rs = pl.ds(g * jg, jg)
        value = mm_packed(mfull[rs, :], inv_a[...], inv_b[...])
        b_out[rs, :] = value
        return value

    def sixth(g, value):
        rs = pl.ds(g * jg, jg)
        for k in range(kl):
            s = jnp.sum(part[k, rs, :] * value, axis=0, keepdims=True)
            acc_ref[pl.ds(k, 1), :] = acc_ref[pl.ds(k, 1), :] + s

    quarter = max(1, blocks // 4)
    owners = 2 * nj * nk
    share = rank // owners

    def owner_at(ia, ja, ka):
        return (jnp.where(ia < middle, 0, nj) + ja) * nk + ka

    def share_of(n):
        return pl.ds(pl.multiple_of(n * share, 8), share)

    me = owner_at(mi, mj, mk)
    gather_cp, spread_cp = [], []
    for ia in (mi, ni - 1 - mi):
        for e in range(nj):
            for f in range(nk):
                if ia is mi and e + f == 0:
                    continue
                where = {"ia": ia, **peer("ja", mj, nj, e), **peer("ka", mk, nk, f)}
                to = owner_at(ia, where["ja"], where["ka"])
                gather_cp.append(
                    planned(g1.at[share_of(to), :], g_in.at[me], g_send.at[0], g_recv.at[0], where)
                )
    for d in range(ni):
        for e in range(nj):
            for f in range(nk):
                if d + e + f:
                    where = {
                        **peer("ia", mi, ni, d), **peer("ja", mj, nj, e), **peer("ka", mk, nk, f)
                    }
                    piece = g3.at[share_of(me), :]
                    spread_cp.append(planned(piece, piece, g_send.at[1], g_recv.at[1], where))

    def own_gram(q):
        @pl.when(is_center)
        def _():
            some = range(q * quarter, q * quarter + quarter)
            known = jnp.concatenate([mfull[own_rows(b, keep, jh), :] for b in some], axis=0)
            gram = mtm(mm_packed(known, inv_a[...], inv_b[...]))
            g1[...] = gram if q == 0 else g1[...] + gram

    def leg(n):
        @pl.when(is_center)
        def _():
            if n == 0:
                for cp in gather_cp:
                    cp.start()
                g_in[me] = g1[share_of(me), :]
            else:
                landed(g_in.at[pl.ds(0, owners - 1)], g_recv.at[0])
                total = g_in[0]
                for m in range(1, owners):
                    total = total + g_in[m]
                g3[share_of(me), :] = total
                for cp in spread_cp:
                    cp.start()

    ahead = min(2, groups)
    for b in range(ahead):
        first(b)
    pl.semaphore_wait(barrier, ni + nj + nk - 3)
    strip = rank // nj
    part_rows = pl.ds(pl.multiple_of(mj * strip, 8), strip)
    ga_in[mi] = ga_loc[part_rows, :]
    for d in range(1, ni):
        remote(
            ga_loc.at[part_rows, :], ga_in.at[mi], ga_send, ga_recv, peer("ia", mi, ni, d)
        )
    for b in range(ahead):
        send_first(b)
    state = {}

    def gram_reduce():
        landed(ga_in.at[pl.ds(0, ni - 1)], ga_recv)
        total = ga_in[0]
        for d in range(1, ni):
            total = total + ga_in[d]
        ga_full[part_rows, :] = total
        for d in range(1, nj):
            rows_here = ga_full.at[part_rows, :]
            remote(rows_here, rows_here, gf_send, gf_recv, peer("ja", mj, nj, d))

    def side_steps():
        landed(ga_full.at[pl.ds(0, (nj - 1) * strip), :], gf_recv)
        h = ga_full[...] * gc_ref[...]
        down, across = scales(h)
        for h in inverse_steps(h * down * across):
            yield
        inv_a[...], inv_b[...] = pack_right(h * down * across)
        yield

    acc_ref[...] = jnp.zeros_like(acc_ref)
    units = rank // PIECE + 1
    side = side_steps()
    left = units

    def advance(count):
        for _ in range(count):
            next(side)

    stages = {
        "second": second,
        "fold": fold,
        "third": third,
        "center_done": center_done,
        "outer_done": outer_done,
        "leg": leg,
    }
    for name, b in plan(blocks, groups, units, 2):
        if name == "first":
            if b >= ahead:
                first(b)
                send_first(b)
        elif name == "gram_reduce":
            gram_reduce()
        elif name == "side":
            if left:
                advance(1)
                left -= 1
        elif name in ("fifth", "own_gram"):
            advance(left)
            left = 0
            if name == "own_gram":
                own_gram(b)
                continue
            value = fifth(b)
            if b + 1 < groups:
                sixth(b, value)
        else:
            stages[name](b)

    sixth(groups - 1, value)
    mc_all[mi * nj + mj] = acc_ref[...]
    for d in range(ni):
        for e in range(nj):
            if d + e:
                where = {**peer("ia", mi, ni, d), **peer("ja", mj, nj, e)}
                slot = mc_all.at[mi * nj + mj]
                remote(slot, slot, mc_send, mc_recv, where)

    @pl.when(is_center)
    def _():
        landed(g3.at[pl.ds(0, rank - share), :], g_recv.at[1])

    @pl.when(jnp.logical_not(is_center))
    def _():
        landed(g3, g_recv.at[1])

    h = ga_full[...] * g3[...]
    down, across = scales(h)
    h = h * down * across
    first_w, second_w = pack_right(inverse(h) * down * across)
    others = mc_all.at[pl.ds(0, ni * nj - 1)]
    settle()

    @pl.when(is_center)
    def _():
        drained(g_in.at[pl.ds(0, owners - 1)], g_send.at[0])
        for cp in spread_cp:
            cp.wait_send()

    drained(others, mc_send)
    landed(others, mc_recv)
    mttkrp_c = mc_all[0]
    for n in range(1, ni * nj):
        mttkrp_c = mttkrp_c + mc_all[n]
    c_out[...] = mm_packed(mttkrp_c, first_w, second_w)[:kl, :]


def pass_on(b_ref, c_ref, b_out, c_out, sems):
    pairs = ((c_ref, c_out), (b_ref, b_out))
    moves = [pltpu.make_async_copy(src, dst, sems.at[n]) for n, (src, dst) in enumerate(pairs)]
    for cp in moves:
        cp.start()
    for cp in moves:
        cp.wait()


def deliver(b, c):
    hbm = pl.BlockSpec(memory_space=pltpu.HBM)
    vmem = pl.BlockSpec(memory_space=pltpu.VMEM)
    return pl.pallas_call(
        pass_on,
        out_shape=(jax.ShapeDtypeStruct(b.shape, b.dtype), jax.ShapeDtypeStruct(c.shape, c.dtype)),
        in_specs=[vmem, vmem],
        out_specs=(hbm, hbm),
        scratch_shapes=[pltpu.SemaphoreType.DMA((2,))],
        compiler_params=pltpu.CompilerParams(vmem_limit_bytes=4 * 1024 * 1024),
    )(b, c)


def body(dims, tensor, factor_a, factor_c, gram_c):
    ni, nj, nk = dims
    rows, kl, il = tensor.shape
    rank = factor_a.shape[1]
    blocks = min(NB, rows // (16 * nk))
    groups = min(8, blocks)
    owners = 2 * nj * nk
    jb = rows // blocks
    jx = jb // nk
    jg = rows // groups
    per = blocks // groups
    kp = -(-kl // 8) * 8
    strip = rank // nj
    f32 = jnp.float32
    dma = pltpu.SemaphoreType.DMA
    vmem = pl.BlockSpec(memory_space=pltpu.VMEM)
    b, c = pl.pallas_call(
        functools.partial(kernel, dims, blocks, groups),
        out_shape=(pltpu.VMEM((rows, rank), f32), pltpu.VMEM((kl, rank), f32)),
        in_specs=[pl.BlockSpec(memory_space=pltpu.HBM)] * 4,
        out_specs=(vmem, vmem),
        scratch_shapes=[
            pltpu.VMEM((kl, rows, il), f32),
            pltpu.VMEM((kl, rows, rank), f32),
            pltpu.VMEM((rows, rank), f32),
            pltpu.VMEM((blocks, nk - 1, jx, rank), f32),
            pltpu.VMEM((blocks, jx, rank), f32),
            pltpu.VMEM((blocks, jx, rank), f32),
            pltpu.VMEM((blocks, jx // 2, rank), f32),
            pltpu.VMEM((rows, rank), f32),
            pltpu.VMEM((rank, rank), f32),
            pltpu.VMEM((ni, strip, rank), f32),
            pltpu.VMEM((rank, rank), f32),
            pltpu.VMEM((rank, rank), f32),
            pltpu.VMEM((owners, rank // owners, rank), f32),
            pltpu.VMEM((rank, rank), f32),
            pltpu.VMEM((ni * nj, kp, rank), f32),
            pltpu.VMEM((2 * rank, 2 * rank), jnp.bfloat16),
            pltpu.VMEM((2 * rank, rank), jnp.bfloat16),
            pltpu.VMEM((kp, rank), f32),
            pltpu.VMEM((il, rank), f32),
            pltpu.VMEM((kl, rank), f32),
            pltpu.VMEM((rank, rank), f32),
            dma((groups,)),
            dma,
            dma((blocks, nk - 1)),
            dma((2,)),
            dma((blocks, 2)),
            dma((2,)),
            dma,
            dma((groups, nk - 1)),
            dma,
            dma,
            dma,
            dma,
            dma((2,)),
            dma((2,)),
            dma,
            dma,
            dma((3,)),
        ],
        compiler_params=pltpu.CompilerParams(
            collective_id=0, has_side_effects=True, vmem_limit_bytes=KL
        ),
    )(tensor, factor_a, factor_c, gram_c)
    return deliver(b, c)


def solution(mesh):
    dims = (mesh.shape["ia"], mesh.shape["ja"], mesh.shape["ka"])
    placed = (P("ja", "ka", "ia"), P("ia", None), P("ka", None), P())
    return jax.shard_map(
        functools.partial(body, dims),
        mesh=mesh,
        in_specs=placed,
        out_specs=(P("ja", None), P("ka", None)),
        check_vma=False,
    )
```

```python
import functools

import jax
import jax.numpy as jnp
from jax import lax
from jax.experimental import pallas as pl
from jax.experimental.pallas import tpu as pltpu
from jax.sharding import PartitionSpec as P

HIGH = lax.Precision.HIGHEST
MESH = pl.DeviceIdType.MESH
PANEL = 64
WARM, FIRST, BEGIN, X_TIME, HOP = 2.0, 3.7, 3.0, 11.4, 2.5
LAG = (3.2, 3.2, 3.2, 3.2, 0.0)
REDUCE_AT, GRAM_AT, UNIT = 8, 12, 0.35
PIECE = 8
NB = 16
LEG = 4.0
SPARE, RAMP = 1.5, 1.0
KL = 56 * 1024 * 1024


def mm(a, b):
    return jnp.dot(a, b, precision=HIGH, preferred_element_type=jnp.float32)


def split3(x):
    a = x.astype(jnp.bfloat16)
    x = x - a.astype(jnp.float32)
    b = x.astype(jnp.bfloat16)
    c = (x - b.astype(jnp.float32)).astype(jnp.bfloat16)
    return a, b, c


def pack_right(w):
    b1, b2, b3 = split3(w)
    top = jnp.concatenate([b1, b2], axis=1)
    return jnp.concatenate([top, top], axis=0), jnp.concatenate([b1, b3], axis=0)


def mm_packed(x, first, second):
    n = second.shape[1]
    a1, a2, a3 = split3(x)
    y = jnp.dot(jnp.concatenate([a1, a2], axis=1), first, preferred_element_type=jnp.float32)
    z = jnp.dot(jnp.concatenate([a3, a1], axis=1), second, preferred_element_type=jnp.float32)
    return y[:, :n] + (y[:, n:] + z)


def mtm(a):
    return lax.dot_general(
        a, a, (((0,), (0,)), ((), ())), precision=HIGH, preferred_element_type=jnp.float32
    )


def take_pivots(rows, q, at):
    n = rows[0].shape[1]
    lane = lax.broadcasted_iota(jnp.int32, (PIECE, n), 1)
    sub = lax.broadcasted_iota(jnp.int32, (PIECE, n), 0)
    lane_row = lax.broadcasted_iota(jnp.int32, (1, n), 1)
    order = [q] + [v for v in range(len(rows)) if v != q]
    cols = {
        v: [jnp.broadcast_to(rows[v][:, at + j : at + j + 1], (PIECE, n)) for j in range(PIECE)]
        for v in order
    }
    x, ahead = rows[q], list(cols[q])
    for t in range(0, PIECE, 2):
        c0, c1 = ahead[t], ahead[t + 1]
        p, r = c0[t : t + 1], c1[t : t + 1]
        u, s = c0[t + 1 : t + 2], c1[t + 1 : t + 2]
        inv = 1.0 / (p * s - r * u)

        def step(y0, y1, kept):
            w0 = (s * y0 - r * y1) * inv
            w1 = (p * y1 - u * y0) * inv
            rest = kept - c0 * w0 - c1 * w1
            return jnp.where(sub == t, w0, jnp.where(sub == t + 1, w1, rest))

        for j in range(t + 2, PIECE):
            y = ahead[j]
            ahead[j] = step(y[t : t + 1], y[t + 1 : t + 2], y)
        here, there = lane_row == at + t, lane_row == at + t + 1
        y0 = jnp.where(here, 1.0, jnp.where(there, 0.0, x[t : t + 1]))
        y1 = jnp.where(here, 0.0, jnp.where(there, 1.0, x[t + 1 : t + 2]))
        x = step(y0, y1, jnp.where((lane == at + t) | (lane == at + t + 1), 0.0, x))
    own = (lane >= at) & (lane < at + PIECE)
    out = list(rows)
    out[q] = x
    for v in order[1:]:
        terms = [cols[v][j] * x[j : j + 1] for j in range(PIECE)]
        while len(terms) > 1:
            terms = [terms[i] + terms[i + 1] for i in range(0, len(terms), 2)]
        out[v] = jnp.where(own, 0.0, rows[v]) - terms[0]
    return out


def inverse_steps(a):
    n = a.shape[0]
    lane = lax.broadcasted_iota(jnp.int32, (n, n), 1)
    sub = lax.broadcasted_iota(jnp.int32, (n, n), 0)
    for base in range(0, n, PANEL):
        rows = [a[base + m : base + m + PIECE] for m in range(0, PANEL, PIECE)]
        for q in range(len(rows)):
            rows = take_pivots(rows, q, base + PIECE * q)
            if q + 1 < len(rows):
                yield None
        pieces = [jnp.zeros((base, n), jnp.float32)] if base else []
        pieces += rows
        if base + PANEL < n:
            pieces.append(jnp.zeros((n - base - PANEL, n), jnp.float32))
        done = jnp.concatenate(pieces, axis=0)
        inside = (lane >= base) & (lane < base + PANEL)
        factor = jnp.where(inside, a, 0.0)
        rest = jnp.where(inside, 0.0, a) - mm_packed(factor, *pack_right(done))
        a = jnp.where((sub >= base) & (sub < base + PANEL), done, rest)
        yield a


def inverse(a):
    for a in inverse_steps(a):
        pass
    return a


def plan(blocks, groups, units, legs):
    quarter = max(1, blocks // 4)
    pace = X_TIME / blocks
    events = []
    ready = [0.0] * blocks
    per = blocks // groups
    for g in range(groups):
        events.append((WARM + FIRST / groups * (g + 1), g * per, "first", g))
    for b in range(blocks):
        t = BEGIN + pace * (b + 1) + HOP
        for n, name in enumerate(("second", "fold", "third", "center_done", "outer_done")):
            events.append((t, b, name, b))
            ready[b] = t
            if name == "third" and b % quarter == quarter - 1:
                events.append((max(t, GRAM_AT + units * UNIT) + 0.1, blocks, "own_gram", b // quarter))
                last = events[-1][0]
            t += LAG[n] * min(1.0, RAMP + (1.0 - RAMP) * b / blocks * 2)
    link = BEGIN + X_TIME
    for b in range(blocks):
        link = max(link, ready[b]) + pace
        if b % per == per - 1:
            events.append((link + HOP + SPARE, b, "fifth", b // per))
    for n in range(legs):
        events.append((last + 0.1 + LEG * n, blocks, "leg", n))
    events.append((REDUCE_AT, blocks, "gram_reduce", None))
    for n in range(units):
        events.append((GRAM_AT + n * UNIT, blocks, "side", None))
    return [(name, b) for _, _, name, b in sorted(events, key=lambda e: e[:2])]


def scales(h):
    n = h.shape[0]
    eye = lax.broadcasted_iota(jnp.int32, (n, n), 1) == lax.broadcasted_iota(jnp.int32, (n, n), 0)
    kept = jnp.where(eye, h, 0.0)
    across = lax.rsqrt(jnp.sum(kept, axis=0, keepdims=True))
    down = lax.rsqrt(jnp.sum(kept, axis=1, keepdims=True))
    return down, across


def kernel(
    dims,
    blocks,
    groups,
    t_hbm,
    a_hbm,
    c_hbm,
    gc_hbm,
    b_out,
    c_out,
    tbuf,
    part,
    mloc,
    xrecv,
    xsum,
    zrecv,
    zhalf,
    mfull,
    ga_loc,
    ga_in,
    ga_full,
    g1,
    g_in,
    g3,
    mc_all,
    inv_a,
    inv_b,
    acc_ref,
    a_ref,
    c_ref,
    gc_ref,
    t_sem,
    x_send,
    x_recv,
    z_send,
    z_recv,
    p_send,
    q_send,
    q_recv,
    ga_send,
    ga_recv,
    gf_send,
    gf_recv,
    g_send,
    g_recv,
    mc_send,
    mc_recv,
    i_sem,
):
    ni, nj, nk = dims
    kl, rows, rank = part.shape
    jb = rows // blocks
    jx = jb // nk
    jg = rows // groups
    per = blocks // groups
    mi, mj, mk = lax.axis_index("ia"), lax.axis_index("ja"), lax.axis_index("ka")

    def peer(axis, me, n, d):
        return {axis: lax.rem(me + d, n)}

    def planned(src, dst, ss, rs, who):
        return pltpu.make_async_remote_copy(
            src_ref=src, dst_ref=dst, send_sem=ss, recv_sem=rs, device_id=who, device_id_type=MESH
        )

    def remote(src, dst, ss, rs, who):
        cp = planned(src, dst, ss, rs, who)
        cp.start()
        return cp

    def drained(ref, sem):
        planned(ref, ref, sem, sem, {"ka": mk}).wait_send()

    def landed(ref, sem):
        planned(ref, ref, sem, sem, {"ka": mk}).wait_recv()

    barrier = pltpu.get_barrier_semaphore()
    for d in range(1, ni):
        pl.semaphore_signal(barrier, inc=1, device_id=peer("ia", mi, ni, d), device_id_type=MESH)
    for d in range(1, nj):
        pl.semaphore_signal(barrier, inc=1, device_id=peer("ja", mj, nj, d), device_id_type=MESH)
    for d in range(1, nk):
        pl.semaphore_signal(barrier, inc=1, device_id=peer("ka", mk, nk, d), device_id_type=MESH)

    icopies = []
    for n, (src, dst) in enumerate(((a_hbm, a_ref), (c_hbm, c_ref), (gc_hbm, gc_ref))):
        cp = pltpu.make_async_copy(src, dst, i_sem.at[n])
        cp.start()
        icopies.append(cp)
    for b in range(groups):
        for k in range(kl):
            rs = pl.ds(b * jg, jg)
            cp = pltpu.make_async_copy(t_hbm.at[rs, k, :], tbuf.at[k, rs, :], t_sem.at[b])
            cp.start()

    for cp in icopies:
        cp.wait()
    a = a_ref[...]
    a_hi = a.astype(jnp.bfloat16)
    a_lo = (a - a_hi.astype(jnp.float32)).astype(jnp.bfloat16)
    weights = jnp.concatenate([a_hi, a_lo], axis=1)

    x_cp, z_cp, p_cp, q_cp = {}, {}, {}, {}
    step = min(256, jg)

    def first(b):
        piece = tbuf.at[:, pl.ds(b * jg, jg), :]
        pltpu.make_async_copy(piece, piece, t_sem.at[b]).wait()

        def chunk(s, carry):
            rs = pl.ds(pl.multiple_of(b * jg + s * step, step), step)
            total = None
            for k in range(kl):
                x = tbuf[k, rs, :]
                hi = x.astype(jnp.bfloat16)
                lo = (x - hi.astype(jnp.float32)).astype(jnp.bfloat16)
                y = jnp.dot(hi, weights, preferred_element_type=jnp.float32) + jnp.dot(
                    lo, weights, preferred_element_type=jnp.float32
                )
                y = y[:, :rank] + y[:, rank:]
                part[k, rs, :] = y
                y = y * c_ref[k : k + 1, :]
                total = y if total is None else total + y
            mloc[rs, :] = total
            return carry

        lax.fori_loop(0, jg // step, chunk, 0)

    def send_first(g):
        for b in range(g * per, g * per + per):
            for d in range(1, nk):
                other = lax.rem(mk + d, nk)
                rs = pl.ds(pl.multiple_of(b * jb + other * jx, 8), jx)
                x_cp[b, d] = remote(
                    mloc.at[rs, :], xrecv.at[b, d - 1], x_send, x_recv.at[b, d - 1],
                    peer("ka", mk, nk, d),
                )

    def own_rows(b, at, size):
        return pl.ds(pl.multiple_of(b * jb + mk * jx + at, 8), size)

    middle = ni // 2
    low_side = mi < middle
    is_center = (mi == middle - 1) | (mi == middle)
    has_outer = (mi > 0) & (mi < ni - 1)
    inward = {"ia": jnp.clip(jnp.where(low_side, mi + 1, mi - 1), 0, ni - 1)}
    outward = {"ia": jnp.clip(jnp.where(low_side, mi - 1, mi + 1), 0, ni - 1)}
    across = {"ia": ni - 1 - mi}
    jh = jx // 2
    keep = jnp.where(low_side, 0, jh)
    give = jh - keep
    fold_cp, part_cp, half_cp, unfold_cp = {}, {}, {}, {}
    for b in range(blocks):
        fold_cp[b] = planned(
            xsum.at[b], zrecv.at[b], z_send.at[0], z_recv.at[b, 0], inward
        )
        part_cp[b] = planned(
            xsum.at[b, pl.ds(pl.multiple_of(give, 8), jh), :], zhalf.at[b],
            z_send.at[1], z_recv.at[b, 1], across,
        )
        rs = own_rows(b, keep, jh)
        half_cp[b] = planned(
            mfull.at[rs, :], mfull.at[rs, :], p_send.at[0], z_recv.at[b, 0], across
        )
        rs = own_rows(b, 0, jx)
        unfold_cp[b] = planned(
            mfull.at[rs, :], mfull.at[rs, :], p_send.at[1], x_recv.at[b, 0], outward
        )
        for d in range(1, nk):
            q_cp[b, d] = planned(
                mfull.at[rs, :], mfull.at[rs, :], q_send, q_recv.at[b // per, d - 1],
                peer("ka", mk, nk, d),
            )

    def second(b):
        total = mloc[own_rows(b, 0, jx), :]
        for d in range(1, nk):
            x_cp[b, d].wait_recv()
            total = total + xrecv[b, d - 1]
        xsum[b] = total

        @pl.when(jnp.logical_not(has_outer))
        def _():
            fold_cp[b].start()

    def fold(b):
        @pl.when(has_outer)
        def _():
            fold_cp[b].wait_recv()
            xsum[b] = xsum[b] + zrecv[b]

            @pl.when(is_center)
            def _():
                part_cp[b].start()

            @pl.when(jnp.logical_not(is_center))
            def _():
                fold_cp[b].start()

    def third(b):
        @pl.when(is_center)
        def _():
            part_cp[b].wait_recv()
            mine = xsum[b, pl.ds(pl.multiple_of(keep, 8), jh), :] + zhalf[b]
            mfull[own_rows(b, keep, jh), :] = mine
            half_cp[b].start()

    def center_done(b):
        @pl.when(is_center)
        def _():
            half_cp[b].wait_recv()
            unfold_cp[b].start()
            for d in range(1, nk):
                q_cp[b, d].start()

    def outer_done(b):
        @pl.when(jnp.logical_not(is_center))
        def _():
            unfold_cp[b].wait_recv()

            @pl.when(has_outer)
            def _():
                unfold_cp[b].start()

            for d in range(1, nk):
                q_cp[b, d].start()

    def settle():
        drained(xrecv, x_send)
        drained(xrecv, q_send)
        drained(ga_in.at[pl.ds(0, ni - 1)], ga_send)
        drained(ga_full.at[pl.ds(0, (nj - 1) * strip), :], gf_send)

        @pl.when(jnp.logical_not(is_center))
        def _():
            drained(zrecv, z_send.at[0])

        @pl.when(is_center)
        def _():
            drained(zhalf, z_send.at[1])
            drained(zhalf, p_send.at[0])

        @pl.when(has_outer)
        def _():
            drained(zrecv, p_send.at[1])

    def fifth(g):
        for d in range(1, nk):
            landed(mfull.at[pl.ds(0, per * jx), :], q_recv.at[g, d - 1])
        rs = pl.ds(g * jg, jg)
        value = mm_packed(mfull[rs, :], inv_a[...], inv_b[...])
        b_out[rs, :] = value
        return value

    def sixth(g, value):
        rs = pl.ds(g * jg, jg)
        for k in range(kl):
            s = jnp.sum(part[k, rs, :] * value, axis=0, keepdims=True)
            acc_ref[pl.ds(k, 1), :] = acc_ref[pl.ds(k, 1), :] + s

    quarter = max(1, blocks // 4)
    owners = 2 * nj * nk
    share = rank // owners

    def owner_at(ia, ja, ka):
        return (jnp.where(ia < middle, 0, nj) + ja) * nk + ka

    def share_of(n):
        return pl.ds(pl.multiple_of(n * share, 8), share)

    me = owner_at(mi, mj, mk)
    gather_cp, spread_cp = [], []
    for ia in (mi, ni - 1 - mi):
        for e in range(nj):
            for f in range(nk):
                if ia is mi and e + f == 0:
                    continue
                where = {"ia": ia, **peer("ja", mj, nj, e), **peer("ka", mk, nk, f)}
                to = owner_at(ia, where["ja"], where["ka"])
                gather_cp.append(
                    planned(g1.at[share_of(to), :], g_in.at[me], g_send.at[0], g_recv.at[0], where)
                )
    for d in range(ni):
        for e in range(nj):
            for f in range(nk):
                if d + e + f:
                    where = {
                        **peer("ia", mi, ni, d), **peer("ja", mj, nj, e), **peer("ka", mk, nk, f)
                    }
                    piece = g3.at[share_of(me), :]
                    spread_cp.append(planned(piece, piece, g_send.at[1], g_recv.at[1], where))

    def own_gram(q):
        @pl.when(is_center)
        def _():
            some = range(q * quarter, q * quarter + quarter)
            known = jnp.concatenate([mfull[own_rows(b, keep, jh), :] for b in some], axis=0)
            gram = mtm(mm_packed(known, inv_a[...], inv_b[...]))
            g1[...] = gram if q == 0 else g1[...] + gram

    def leg(n):
        @pl.when(is_center)
        def _():
            if n == 0:
                for cp in gather_cp:
                    cp.start()
                g_in[me] = g1[share_of(me), :]
            else:
                landed(g_in.at[pl.ds(0, owners - 1)], g_recv.at[0])
                total = g_in[0]
                for m in range(1, owners):
                    total = total + g_in[m]
                g3[share_of(me), :] = total
                for cp in spread_cp:
                    cp.start()

    ahead = min(1, groups)
    for b in range(ahead):
        first(b)
    pl.semaphore_wait(barrier, ni + nj + nk - 3)
    for b in range(ahead):
        send_first(b)
    ga_loc[...] = mtm(a)
    strip = rank // nj
    part_rows = pl.ds(pl.multiple_of(mj * strip, 8), strip)
    ga_in[mi] = ga_loc[part_rows, :]
    for d in range(1, ni):
        remote(
            ga_loc.at[part_rows, :], ga_in.at[mi], ga_send, ga_recv, peer("ia", mi, ni, d)
        )
    state = {}

    def gram_reduce():
        landed(ga_in.at[pl.ds(0, ni - 1)], ga_recv)
        total = ga_in[0]
        for d in range(1, ni):
            total = total + ga_in[d]
        ga_full[part_rows, :] = total
        for d in range(1, nj):
            rows_here = ga_full.at[part_rows, :]
            remote(rows_here, rows_here, gf_send, gf_recv, peer("ja", mj, nj, d))

    def side_steps():
        landed(ga_full.at[pl.ds(0, (nj - 1) * strip), :], gf_recv)
        h = ga_full[...] * gc_ref[...]
        down, across = scales(h)
        for h in inverse_steps(h * down * across):
            yield
        inv_a[...], inv_b[...] = pack_right(h * down * across)
        yield

    acc_ref[...] = jnp.zeros_like(acc_ref)
    units = rank // PIECE + 1
    side = side_steps()
    left = units

    def advance(count):
        for _ in range(count):
            next(side)

    stages = {
        "second": second,
        "fold": fold,
        "third": third,
        "center_done": center_done,
        "outer_done": outer_done,
        "leg": leg,
    }
    for name, b in plan(blocks, groups, units, 2):
        if name == "first":
            if b >= ahead:
                first(b)
                send_first(b)
        elif name == "gram_reduce":
            gram_reduce()
        elif name == "side":
            if left:
                advance(1)
                left -= 1
        elif name in ("fifth", "own_gram"):
            advance(left)
            left = 0
            if name == "own_gram":
                own_gram(b)
                continue
            value = fifth(b)
            if b + 1 < groups:
                sixth(b, value)
        else:
            stages[name](b)

    sixth(groups - 1, value)
    mc_all[mi * nj + mj] = acc_ref[...]
    for d in range(ni):
        for e in range(nj):
            if d + e:
                where = {**peer("ia", mi, ni, d), **peer("ja", mj, nj, e)}
                slot = mc_all.at[mi * nj + mj]
                remote(slot, slot, mc_send, mc_recv, where)

    @pl.when(is_center)
    def _():
        landed(g3.at[pl.ds(0, rank - share), :], g_recv.at[1])

    @pl.when(jnp.logical_not(is_center))
    def _():
        landed(g3, g_recv.at[1])

    h = ga_full[...] * g3[...]
    down, across = scales(h)
    h = h * down * across
    first_w, second_w = pack_right(inverse(h) * down * across)
    others = mc_all.at[pl.ds(0, ni * nj - 1)]
    settle()

    @pl.when(is_center)
    def _():
        drained(g_in.at[pl.ds(0, owners - 1)], g_send.at[0])
        for cp in spread_cp:
            cp.wait_send()

    drained(others, mc_send)
    landed(others, mc_recv)
    mttkrp_c = mc_all[0]
    for n in range(1, ni * nj):
        mttkrp_c = mttkrp_c + mc_all[n]
    c_out[...] = mm_packed(mttkrp_c, first_w, second_w)[:kl, :]


def pass_on(b_ref, c_ref, b_out, c_out, sems):
    pairs = ((c_ref, c_out), (b_ref, b_out))
    moves = [pltpu.make_async_copy(src, dst, sems.at[n]) for n, (src, dst) in enumerate(pairs)]
    for cp in moves:
        cp.start()
    for cp in moves:
        cp.wait()


def deliver(b, c):
    hbm = pl.BlockSpec(memory_space=pltpu.HBM)
    vmem = pl.BlockSpec(memory_space=pltpu.VMEM)
    return pl.pallas_call(
        pass_on,
        out_shape=(jax.ShapeDtypeStruct(b.shape, b.dtype), jax.ShapeDtypeStruct(c.shape, c.dtype)),
        in_specs=[vmem, vmem],
        out_specs=(hbm, hbm),
        scratch_shapes=[pltpu.SemaphoreType.DMA((2,))],
        compiler_params=pltpu.CompilerParams(vmem_limit_bytes=4 * 1024 * 1024),
    )(b, c)


def body(dims, tensor, factor_a, factor_c, gram_c):
    ni, nj, nk = dims
    rows, kl, il = tensor.shape
    rank = factor_a.shape[1]
    blocks = min(NB, rows // (16 * nk))
    groups = min(8, blocks)
    owners = 2 * nj * nk
    jb = rows // blocks
    jx = jb // nk
    jg = rows // groups
    per = blocks // groups
    kp = -(-kl // 8) * 8
    strip = rank // nj
    f32 = jnp.float32
    dma = pltpu.SemaphoreType.DMA
    vmem = pl.BlockSpec(memory_space=pltpu.VMEM)
    b, c = pl.pallas_call(
        functools.partial(kernel, dims, blocks, groups),
        out_shape=(pltpu.VMEM((rows, rank), f32), pltpu.VMEM((kl, rank), f32)),
        in_specs=[pl.BlockSpec(memory_space=pltpu.HBM)] * 4,
        out_specs=(vmem, vmem),
        scratch_shapes=[
            pltpu.VMEM((kl, rows, il), f32),
            pltpu.VMEM((kl, rows, rank), f32),
            pltpu.VMEM((rows, rank), f32),
            pltpu.VMEM((blocks, nk - 1, jx, rank), f32),
            pltpu.VMEM((blocks, jx, rank), f32),
            pltpu.VMEM((blocks, jx, rank), f32),
            pltpu.VMEM((blocks, jx // 2, rank), f32),
            pltpu.VMEM((rows, rank), f32),
            pltpu.VMEM((rank, rank), f32),
            pltpu.VMEM((ni, strip, rank), f32),
            pltpu.VMEM((rank, rank), f32),
            pltpu.VMEM((rank, rank), f32),
            pltpu.VMEM((owners, rank // owners, rank), f32),
            pltpu.VMEM((rank, rank), f32),
            pltpu.VMEM((ni * nj, kp, rank), f32),
            pltpu.VMEM((2 * rank, 2 * rank), jnp.bfloat16),
            pltpu.VMEM((2 * rank, rank), jnp.bfloat16),
            pltpu.VMEM((kp, rank), f32),
            pltpu.VMEM((il, rank), f32),
            pltpu.VMEM((kl, rank), f32),
            pltpu.VMEM((rank, rank), f32),
            dma((groups,)),
            dma,
            dma((blocks, nk - 1)),
            dma((2,)),
            dma((blocks, 2)),
            dma((2,)),
            dma,
            dma((groups, nk - 1)),
            dma,
            dma,
            dma,
            dma,
            dma((2,)),
            dma((2,)),
            dma,
            dma,
            dma((3,)),
        ],
        compiler_params=pltpu.CompilerParams(
            collective_id=0, has_side_effects=True, vmem_limit_bytes=KL
        ),
    )(tensor, factor_a, factor_c, gram_c)
    return deliver(b, c)


def solution(mesh):
    dims = (mesh.shape["ia"], mesh.shape["ja"], mesh.shape["ka"])
    placed = (P("ja", "ka", "ia"), P("ia", None), P("ka", None), P())
    return jax.shard_map(
        functools.partial(body, dims),
        mesh=mesh,
        in_specs=placed,
        out_specs=(P("ja", None), P("ka", None)),
        check_vma=False,
    )
```
